32 devices in a mesh: slab: 8 (over y, x, core), tile: 4 (over z).
Axes of the slice: x: 2, y: 2, z: 4, core: 2. Of those that a mesh axis runs over, the one named last changes fastest.
Arguments:
- particle_features: bfloat16 [6, 131072], P(None, ('slab', 'tile')), may hold values from -6 to 6
- destination: int32 [131072, 1], P(('slab', 'tile')), may hold values from 0 to 7; in each aligned block of 4096 rows (0 to 4095, 4096 to 8191, ...) at most 2048 rows name the same one
- cell_index: int32 [131072], P(('slab', 'tile')), may hold values from 0 to 16383
- offset_code: int32 [131072], P(('slab', 'tile')), may hold values from 0 to 262143
- live_count: int32 [32], P(('slab', 'tile')), may hold values from 2048 to 4096, as said below
- lift_weight: bfloat16 [3, 3, 64, 18], replicated, may hold values from -0.5 to 0.5
- fine_weight: bfloat16 [3, 3, 64, 192], replicated, may hold values from -0.15625 to 0.15625
- down_weight: bfloat16 [2, 2, 2, 256, 64], replicated, may hold values from -0.25 to 0.25
- coarse_weight: bfloat16 [3, 3, 256, 768], replicated, may hold values from -0.078125 to 0.078125
- up_weight: bfloat16 [2, 2, 2, 64, 256], replicated, may hold values from -0.375 to 0.375
- merge_weight: bfloat16 [3, 3, 64, 192], replicated, may hold values from -0.15625 to 0.15625
- head_weight: bfloat16 [3, 64], replicated, may hold values from -0.75 to 0.75
Outputs:
- displacement: float32 [3, 32, 32, 128], P(None, 'slab', 'tile')
The draws below stay inside these ranges and needn't reach their ends.
Inputs may be any that keep to these rules, and one draw needn't show every extreme that they name: `destination`: among the rows of one device, at most 2048 name the same slab; some slab is named by exactly 2048 of them. `live_count`: some device has all 4096 rows live.
All inputs are finite; a program needn't handle non-finite values.
Results may differ from the reference program's by a relative error of at most 0.024.
Values may be sent and summed in bfloat16 or wider, within the bound.
A program may use at most 192 MiB of HBM per device.

```python
import math
import jax
import jax.numpy as jnp
import numpy as np
from jax import lax

ATTR = 6
C0 = 64
C1 = 256
C_OUT = 3
NX = 128
CZ = 4
NDEV = 32
NY = 32
NZ = 32
P_DEV = 4096
CAP = 2048
PARTICLES = 131072
N_SLAB = 8


def draw_live_count(key, part):
    first_key, second_key = jax.random.split(jax.random.fold_in(key, 17))
    counts = jax.random.randint(first_key, (NDEV,), P_DEV // 2, P_DEV + 1)
    chosen = jax.random.randint(second_key, (), 0, NDEV)
    return jnp.where(jnp.arange(NDEV) == chosen, P_DEV, counts).astype(jnp.int32)


def touch_ends(result, rng, least, top_value):
    index_at = [jax.random.randint(jax.random.fold_in(rng, axis), (), 0, length) for axis, length in enumerate(result.shape)]
    main_axis = result.shape.index(max(result.shape))
    next_to = index_at[:main_axis] + [(index_at[main_axis] + 1) % result.shape[main_axis]] + index_at[main_axis + 1:]
    return result.at[tuple(index_at)].set(least).at[tuple(next_to)].set(top_value)


def steps_of(key, shape, pieces, low, high):
    def one(dim, blocks):
        draws = jax.random.uniform(jax.random.fold_in(jax.random.fold_in(key, 6), dim), (blocks,), jnp.float32, low / len(pieces), high / len(pieces))
        return jnp.repeat(jnp.exp(draws), shape[dim] // blocks).reshape((-1,) + (1,) * (len(shape) - dim - 1))

    factor_of = one(*pieces[0])
    for cut in pieces[1:]:
        factor_of = factor_of * one(*cut)
    return factor_of


def deal_out(own_key, own, number, rows, number_of, top, bound, skew):
    ranking = jax.random.permutation(own_key, number_of)
    crowded, usual = shares(number_of, rows * top, bound, skew, True), shares(number_of, rows * top, bound, skew, False)
    places = jnp.arange(number_of)

    def named(sizes, offset_by):
        used = int((sizes > 0).sum())
        fixed = max(1, used // 4)
        passed = fixed + (places - fixed + offset_by * (used - fixed)) % max(1, number_of - fixed)
        return jnp.zeros((number_of,), jnp.int32).at[ranking[jnp.where(places < fixed, places, passed)]].set(jnp.asarray(sizes, jnp.int32))

    sizes = jnp.where(number % 4 == 0, named(crowded, number // 4), named(usual, number - number // 4 - 1))
    mixed = jax.random.permutation(jax.random.fold_in(own, 3), number_of)
    donor, taker = mixed[0:number_of // 2 * 2:2], mixed[1:number_of // 2 * 2:2]
    slack = jnp.minimum(sizes[donor] - 1, bound - sizes[taker]) // 2
    slack = jnp.where((donor == ranking[0]) | (taker == ranking[0]) | (sizes[taker] == 0), 0, jnp.maximum(slack, 0))
    passed = jax.random.randint(jax.random.fold_in(own, 4), (number_of // 2,), 0, 1 << 20) % (slack + 1)
    sizes = sizes.at[donor].add(-passed).at[taker].add(passed)
    items = jnp.searchsorted(jnp.cumsum(sizes), jnp.arange(rows * top), side="right").astype(jnp.int32)
    table = items.reshape(top, rows).T
    table = table[jax.random.permutation(jax.random.fold_in(own, 1), rows)]
    offset_by = jax.random.randint(jax.random.fold_in(own, 2), (rows, 1), 0, top)
    return jnp.take_along_axis(table, (jnp.arange(top)[None, :] + offset_by) % top, axis=1)


def shares(count, total, reach, skew, full):
    portions = [(1 << 20) // math.isqrt(standing ** skew) + 1 for standing in range(1, count + 1)]
    largest = reach if full else min(reach, max(-(-total // count), total * portions[0] // sum(portions)))
    least = 1 if total - largest >= count - 1 else 0
    given, rest = [largest] + [least] * (count - 1), total - largest - least * (count - 1)
    while rest > 0:
        candidates = [i for i in range(1, count) if given[i] < largest] or [i for i in range(1, count) if given[i] < reach]
        whole, remaining = sum([portions[i] for i in candidates]), rest
        for i in candidates:
            extra = min(reach - given[i], max(1, remaining * portions[i] // whole), rest)
            given[i] = given[i] + extra
            rest = rest - extra
    return np.array(given)


def noise(key, shape, deviation, most, cuts=(), kind=jnp.bfloat16):
    factor_of = steps_of(key, shape, cuts, -0.22, 0.18) if cuts else 1.0
    array = jax.random.normal(key, shape, jnp.float32) * deviation * factor_of
    return jnp.minimum(jnp.maximum(array, -most), most).astype(kind)


def setup_inputs(seed: int = 0) -> dict:
    seeds = jax.random.split(jax.random.key(seed), 13)
    particle_features = noise(seeds[0], (ATTR, PARTICLES), 1.0, 6.0, ((1, 32),))
    destination_keys = jax.random.split(jax.random.fold_in(seeds[1], 1), PARTICLES // P_DEV)
    destination_turns = jax.random.permutation(jax.random.fold_in(seeds[1], 3), PARTICLES // P_DEV)
    destination = jax.vmap(lambda own, number: deal_out(jax.random.fold_in(seeds[1], 2), own, number, P_DEV, N_SLAB, 1, CAP, 2))(destination_keys, destination_turns).reshape((PARTICLES, 1))
    cell_index = touch_ends(jax.random.randint(seeds[2], (PARTICLES,), 0, CZ * NY * NX), jax.random.fold_in(seeds[2], 1), 0, (CZ * NY * NX) - 1).astype(jnp.int32)
    offset_code = touch_ends(jax.random.randint(seeds[3], (PARTICLES,), 0, 262144), jax.random.fold_in(seeds[3], 1), 0, 262143).astype(jnp.int32)
    live_count = draw_live_count(jax.random.fold_in(seeds[12], 71), 0)
    lift_weight = noise(seeds[5], (3, 3, C0, 3 * ATTR), (27 * ATTR) ** -0.5, 0.5)
    fine_weight = noise(seeds[6], (3, 3, C0, 3 * C0), (27 * C0) ** -0.5, 0.15625)
    down_weight = noise(seeds[7], (2, 2, 2, C1, C0), (8 * C0) ** -0.5, 0.25)
    coarse_weight = noise(seeds[8], (3, 3, C1, 3 * C1), (27 * C1) ** -0.5, 0.078125)
    up_weight = noise(seeds[9], (2, 2, 2, C0, C1), C1 ** -0.5, 0.375)
    merge_weight = noise(seeds[10], (3, 3, C0, 3 * C0), (27 * C0) ** -0.5, 0.15625)
    head_weight = noise(seeds[11], (C_OUT, C0), C0 ** -0.5, 0.75)
    return dict(particle_features=particle_features, destination=destination, cell_index=cell_index, offset_code=offset_code, live_count=live_count, lift_weight=lift_weight, fine_weight=fine_weight, down_weight=down_weight, coarse_weight=coarse_weight, up_weight=up_weight, merge_weight=merge_weight, head_weight=head_weight)


slope = 0.1


def act(values):
    return jnp.maximum(values, slope * values)


def conv_full(field, weight):
    stacked = jnp.concatenate([jnp.roll(field, 1, 3), field, jnp.roll(field, -1, 3)], 0)
    padded = jnp.concatenate([stacked[:, -1:], stacked, stacked[:, :1]], 1)
    wide = weight.astype(jnp.float32)

    def plane(index):
        block = lax.dynamic_slice_in_dim(padded, index, 3, 1).astype(jnp.float32)
        total = jnp.zeros((weight.shape[2], field.shape[2], field.shape[3]), jnp.float32)
        for a in range(3):
            for b in range(3):
                total = total + jnp.einsum('oi,iyx->oyx', wide[a, b], jnp.roll(block[:, a], 1 - b, 1))
        return total

    planes = lax.map(plane, jnp.arange(field.shape[1], dtype=jnp.int32))
    return jnp.transpose(planes, (1, 0, 2, 3))


def deposit_full(particle_features, destination, cell_index, offset_code, live_count):
    rows = jnp.arange(PARTICLES, dtype=jnp.int32)
    live = ((rows % P_DEV) < jnp.repeat(live_count, P_DEV)).astype(jnp.float32)
    values = particle_features.astype(jnp.float32) * live[None, :]
    plane_z = destination[:, 0] * CZ + cell_index // (NY * NX)
    row_y = (cell_index // NX) % NY
    col_x = cell_index % NX
    frac_z = ((offset_code // 4096) % 64).astype(jnp.float32) / 64.0
    frac_y = ((offset_code // 64) % 64).astype(jnp.float32) / 64.0
    frac_x = (offset_code % 64).astype(jnp.float32) / 64.0
    field = jnp.zeros((ATTR, NZ * NY * NX), jnp.float32)
    for a in range(2):
        for b in range(2):
            for k in range(2):
                weight_z = frac_z if a else 1.0 - frac_z
                weight_y = frac_y if b else 1.0 - frac_y
                weight_x = frac_x if k else 1.0 - frac_x
                corner = weight_z * weight_y * weight_x
                target = ((plane_z + a) % NZ) * (NY * NX) + ((row_y + b) % NY) * NX + (col_x + k) % NX
                field = field.at[:, target].add(values * corner[None, :])
    return field.reshape(ATTR, NZ, NY, NX)


def reference(particle_features, destination, cell_index, offset_code, live_count, lift_weight, fine_weight, down_weight, coarse_weight, up_weight, merge_weight, head_weight):
    grid = deposit_full(particle_features, destination, cell_index, offset_code, live_count).astype(jnp.bfloat16)
    first = act(conv_full(grid, lift_weight)).astype(jnp.bfloat16)
    second = act(conv_full(first, fine_weight)).astype(jnp.bfloat16)
    blocks = second.astype(jnp.float32).reshape(C0, NZ // 2, 2, NY // 2, 2, NX // 2, 2)
    lowered = act(jnp.einsum('abkoc,czaybxk->ozyx', down_weight.astype(jnp.float32), blocks)).astype(jnp.bfloat16)
    coarse = act(conv_full(lowered, coarse_weight)).astype(jnp.bfloat16)
    raised = jnp.einsum('abkoc,czyx->ozaybxk', up_weight.astype(jnp.float32), coarse.astype(jnp.float32)).reshape(C0, NZ, NY, NX)
    joined = (second.astype(jnp.float32) + raised).astype(jnp.bfloat16)
    merged = act(conv_full(joined, merge_weight)).astype(jnp.bfloat16)
    return jnp.einsum('oc,czyx->ozyx', head_weight.astype(jnp.float32), merged.astype(jnp.float32))
```

```python
import functools

import jax
import jax.numpy as jnp
from jax import lax
from jax.experimental import pallas as pl
from jax.experimental.pallas import tpu as pltpu
from jax.sharding import PartitionSpec as P

NX = 128
YT = 8
CZ = 4


slope = 0.1


def with_halo(block, sides, width):
    for axis, dim in sides:
        count = lax.axis_size(axis)
        forward = [(i, i + 1) for i in range(count - 1)]
        forward.append((count - 1, 0))
        backward = [(target, source) for source, target in forward]
        low = lax.ppermute(
            lax.slice_in_dim(block, block.shape[dim] - width, None, axis=dim), axis, forward
        )
        high = lax.ppermute(lax.slice_in_dim(block, 0, width, axis=dim), axis, backward)
        block = jnp.concatenate([low, block, high], axis=dim)
    return block


def act(values):
    return jnp.maximum(values, slope * values)


def conv_rim(padded, weight):
    stacked = jnp.concatenate([jnp.roll(padded, 1, 3), padded, jnp.roll(padded, -1, 3)], 0)
    out_z = padded.shape[1] - 2
    out_y = padded.shape[2] - 2
    total = jnp.zeros((weight.shape[2], out_z, out_y, padded.shape[3]), jnp.float32)
    for a in range(3):
        for b in range(3):
            total = total + jnp.einsum(
                "oi,izyx->ozyx",
                weight[a, b],
                stacked[:, a : a + out_z, b : b + out_y],
                preferred_element_type=jnp.float32,
            )
    return total


GROUP = 4
CHUNK = 512


def deposit_kernel(slabs, tiles, feat_ref, dest_ref, cell_ref, code_ref, live_ref, out_ref, right, acc):
    group = pl.program_id(0)
    rows = feat_ref.shape[1]
    attrs = feat_ref.shape[0]
    ny = tiles * YT
    nz = slabs * CZ
    f32 = jnp.float32

    @pl.when(group == 0)
    def _():
        def build(j, carry):
            at = pl.ds(pl.multiple_of(j * CHUNK, CHUNK), CHUNK)
            cells = cell_ref[:, at]
            codes = code_ref[:, at]
            lane = lax.broadcasted_iota(jnp.int32, (1, CHUNK), 1) + j * CHUNK
            live = lane < live_ref[0]
            feats = jnp.where(live, feat_ref[:, at].astype(f32), 0.0)
            frac = (codes & 63).astype(f32) * (1.0 / 64.0)
            col = cells & (NX - 1)
            nxt = (col + 1) & (NX - 1)
            xs = lax.broadcasted_iota(jnp.int32, (NX, CHUNK), 0)
            wx = jnp.where(xs == col, 1.0 - frac, 0.0) + jnp.where(xs == nxt, frac, 0.0)
            for c in range(attrs):
                right[c * NX : (c + 1) * NX, at] = (wx * feats[c : c + 1, :]).astype(jnp.bfloat16)
            return carry

        lax.fori_loop(0, rows // CHUNK, build, 0)

    def step(j, carry):
        at = pl.ds(pl.multiple_of(j * CHUNK, CHUNK), CHUNK)
        cells = cell_ref[:, at]
        codes = code_ref[:, at]
        fz = ((codes >> 12) & 63).astype(f32) * (1.0 / 64.0)
        fy = ((codes >> 6) & 63).astype(f32) * (1.0 / 64.0)
        row = cells // NX
        y0 = row % ny
        z0 = dest_ref[:, at] * CZ + row // ny
        y1 = (y0 + 1) % ny
        z1 = (z0 + 1) % nz
        ys = lax.broadcasted_iota(jnp.int32, (ny, CHUNK), 0)
        wy = jnp.where(ys == y0, 1.0 - fy, 0.0) + jnp.where(ys == y1, fy, 0.0)
        zs = lax.broadcasted_iota(jnp.int32, (GROUP * CZ, CHUNK), 0) + group * GROUP * CZ
        wz = jnp.where(zs == z0, 1.0 - fz, 0.0) + jnp.where(zs == z1, fz, 0.0)
        pieces = []
        for s in range(GROUP):
            for t in range(tiles):
                for z in range(CZ):
                    k = s * CZ + z
                    pieces.append(wz[k : k + 1, :] * wy[t * YT : (t + 1) * YT, :])
        left = jnp.concatenate(pieces, 0).astype(jnp.bfloat16)
        part = lax.dot_general(
            left, right[:, at], (((1,), (1,)), ((), ())), preferred_element_type=f32
        )

        @pl.when(j == 0)
        def _():
            acc[...] = part

        @pl.when(j > 0)
        def _():
            acc[...] += part

        return carry

    lax.fori_loop(0, rows // CHUNK, step, 0)
    size = CZ * YT
    for s in range(GROUP):
        for t in range(tiles):
            k = (s * tiles + t) * size
            for c in range(attrs):
                out_ref[s, t, c] = acc[k : k + size, c * NX : (c + 1) * NX].astype(jnp.bfloat16)


def deposit(features, destination, cell_index, offset_code, live_count, slabs, tiles):
    attrs, rows = features.shape
    size = CZ * YT
    whole = lambda shape: pl.BlockSpec(shape, lambda g: (0, 0))
    return pl.pallas_call(
        functools.partial(deposit_kernel, slabs, tiles),
        grid=(slabs // GROUP,),
        in_specs=[
            whole((attrs, rows)),
            whole((1, rows)),
            whole((1, rows)),
            whole((1, rows)),
            pl.BlockSpec(memory_space=pltpu.SMEM),
        ],
        out_specs=pl.BlockSpec((GROUP, tiles, attrs, size, NX), lambda g: (g, 0, 0, 0, 0)),
        out_shape=jax.ShapeDtypeStruct((slabs, tiles, attrs, size, NX), jnp.bfloat16),
        scratch_shapes=[
            pltpu.VMEM((attrs * NX, rows), jnp.bfloat16),
            pltpu.VMEM((GROUP * tiles * size, attrs * NX), jnp.float32),
        ],
        compiler_params=pltpu.CompilerParams(vmem_limit_bytes=48 << 20),
        name="deposit",
    )(
        features,
        destination.reshape(1, rows),
        cell_index.reshape(1, rows),
        offset_code.reshape(1, rows),
        live_count,
    )


def body(
    particle_features,
    destination,
    cell_index,
    offset_code,
    live_count,
    lift_weight,
    fine_weight,
    down_weight,
    coarse_weight,
    up_weight,
    merge_weight,
    head_weight,
):
    slabs = lax.axis_size("slab")
    tiles = lax.axis_size("tile")
    field = deposit(
        particle_features, destination, cell_index, offset_code, live_count, slabs, tiles
    )
    field = lax.all_to_all(field, "slab", split_axis=0, concat_axis=0, tiled=True)
    field = jnp.sum(field.astype(jnp.float32), 0).astype(jnp.bfloat16)
    field = lax.all_to_all(field, "tile", split_axis=0, concat_axis=0, tiled=True)
    grid = jnp.sum(field.astype(jnp.float32), 0).astype(jnp.bfloat16)
    grid = grid.reshape(grid.shape[0], CZ, YT, NX)
    padded = with_halo(grid, (("slab", 1), ("tile", 2)), 2)
    first_padded = act(conv_rim(padded, lift_weight)).astype(jnp.bfloat16)
    second = act(conv_rim(first_padded, fine_weight)).astype(jnp.bfloat16)
    channels, planes, width_y, width_x = second.shape
    blocks = second.reshape(channels, planes // 2, 2, width_y // 2, 2, width_x // 2, 2)
    lowered = act(
        jnp.einsum("abkoc,czaybxk->ozyx", down_weight, blocks, preferred_element_type=jnp.float32)
    ).astype(jnp.bfloat16)
    lowered_padded = with_halo(lowered, (("slab", 1), ("tile", 2)), 1)
    coarse = act(conv_rim(lowered_padded, coarse_weight)).astype(jnp.bfloat16)
    raised = jnp.einsum(
        "abkoc,czyx->ozaybxk", up_weight, coarse, preferred_element_type=jnp.float32
    ).reshape(up_weight.shape[3], planes, width_y, width_x)
    joined = (second.astype(jnp.float32) + raised).astype(jnp.bfloat16)
    joined_padded = with_halo(joined, (("slab", 1), ("tile", 2)), 1)
    merged = act(conv_rim(joined_padded, merge_weight)).astype(jnp.bfloat16)
    return jnp.einsum("oc,czyx->ozyx", head_weight, merged, preferred_element_type=jnp.float32)


def solution(mesh):
    placed = (
        P(None, ("slab", "tile")),
        P(("slab", "tile"), None),
        P(("slab", "tile")),
        P(("slab", "tile")),
        P(("slab", "tile")),
        P(),
        P(),
        P(),
        P(),
        P(),
        P(),
        P(),
    )
    return jax.shard_map(
        body, mesh=mesh, in_specs=placed, out_specs=P(None, "slab", "tile", None), check_vma=False
    )
```

```python
import functools

import jax
import jax.numpy as jnp
from jax import lax
from jax.experimental import pallas as pl
from jax.experimental.pallas import tpu as pltpu
from jax.sharding import PartitionSpec as P

NX = 128
YT = 8
CZ = 4


slope = 0.1


BF16 = jnp.bfloat16
F32 = jnp.float32
MESH = pl.DeviceIdType.MESH
SIDES = [(dz, dy) for dz in (-1, 0, 1) for dy in (-1, 0, 1) if dz or dy]


def act(values):
    return jnp.maximum(values, slope * values)


def dot(left, right):
    return jnp.dot(left, right, preferred_element_type=F32)


def neighbour(dz, dy):
    slabs, tiles = lax.axis_size("slab"), lax.axis_size("tile")
    return (
        lax.rem(lax.axis_index("slab") + (dz + slabs), slabs),
        lax.rem(lax.axis_index("tile") + (dy + tiles), tiles),
    )


def greet(devices):
    barrier = pltpu.get_barrier_semaphore()
    for device in devices:
        pl.semaphore_signal(barrier, inc=1, device_id=device, device_id_type=MESH)
    pl.semaphore_wait(barrier, len(devices))


def span(shift, size, width):
    if shift > 0:
        return pl.ds(size - width, width), pl.ds(0, width)
    if shift < 0:
        return pl.ds(0, width), pl.ds(size + width, width)
    return pl.ds(0, size), pl.ds(width, size)


def exchange(block, padded, width, send, recv):
    planes, rows = block.shape[:2]
    copies = []
    for n, (dz, dy) in enumerate(SIDES):
        from_z, to_z = span(dz, planes, width)
        from_y, to_y = span(dy, rows, width)
        copies.append(
            pltpu.make_async_remote_copy(
                src_ref=block.at[from_z, from_y],
                dst_ref=padded.at[to_z, to_y],
                send_sem=send.at[n],
                recv_sem=recv.at[n],
                device_id=neighbour(dz, dy),
                device_id_type=MESH,
            )
        )
    for copy in copies:
        copy.start()
    padded[pl.ds(width, planes), pl.ds(width, rows)] = block[...]
    for copy in copies:
        copy.wait()


def halo_kernel(width, block, padded, send, recv):
    greet([neighbour(dz, dy) for dz, dy in SIDES])
    exchange(block, padded, width, send, recv)


def with_halo(block, width, number):
    planes, rows, depth, lanes = block.shape
    return pl.pallas_call(
        functools.partial(halo_kernel, width),
        in_specs=[pl.BlockSpec(memory_space=pltpu.VMEM)],
        out_specs=pl.BlockSpec(memory_space=pltpu.VMEM),
        out_shape=jax.ShapeDtypeStruct(
            (planes + 2 * width, rows + 2 * width, depth, lanes), block.dtype
        ),
        scratch_shapes=[pltpu.SemaphoreType.DMA((8,)), pltpu.SemaphoreType.DMA((8,))],
        compiler_params=pltpu.CompilerParams(
            collective_id=number, has_side_effects=True, vmem_limit_bytes=32 << 20
        ),
        name=f"halo{number}",
    )(block)


def reduce_kernel(bits, field, padded, *scratch):
    tiles = lax.axis_size("tile")
    slab, tile = lax.axis_index("slab"), lax.axis_index("tile")
    half = tiles // 2
    mine = [slab // 2**b % 2 for b in range(bits)]
    partner = [(slab + 2**b * (1 - 2 * mine[b]), tile) for b in range(bits)]
    ahead = [(slab, lax.rem(tile + d, tiles)) for d in range(1, tiles)]
    greet(partner + ahead + [neighbour(dz, dy) for dz, dy in SIDES])
    gets, sums = scratch[: 2 * bits], scratch[2 * bits : 4 * bits]
    last, block, send, recv, send_z, recv_z, send_h, recv_h, whole = scratch[4 * bits :]

    def start(source, target, sem, device):
        copy = pltpu.make_async_remote_copy(
            src_ref=source,
            dst_ref=target,
            send_sem=send.at[sem],
            recv_sem=recv.at[sem],
            device_id=device,
            device_id_type=MESH,
        )
        copy.start()
        return copy

    orders = [[0] + list(range(1, bits)), [0] + list(range(bits - 1, 0, -1))]
    left = [list(range(bits - 1, -1, -1)) for _ in range(2)]
    here = [None, None]
    for stage in range(bits):
        copies = []
        for h in range(2):
            b = orders[h][stage]
            at = (slice(None),) * left[h].index(b)
            parts = pl.ds(h * half, half)
            if stage == 0:
                away = field.at[at + (1 - mine[b], parts)]
            else:
                away = here[h].at[at + (1 - mine[b],)]
            copies.append(start(away, gets[2 * stage + h], 2 * stage + h, partner[b]))
        for h in range(2):
            b = orders[h][stage]
            at = (slice(None),) * left[h].index(b)
            parts = pl.ds(h * half, half)
            copies[h].wait()
            if stage == 0:
                own = field[at + (mine[b], parts)]
            else:
                own = here[h][at + (mine[b],)]
            total = own.astype(F32) + gets[2 * stage + h][...].astype(F32)
            sums[2 * stage + h][...] = total.astype(BF16)
            here[h] = sums[2 * stage + h]
            left[h].remove(b)
    whole[pl.ds(0, half)] = here[0][...]
    whole[pl.ds(half, half)] = here[1][...]
    copies = []
    for d in range(1, tiles):
        copy = pltpu.make_async_remote_copy(
            src_ref=whole.at[lax.rem(tile + d, tiles)],
            dst_ref=last.at[d - 1],
            send_sem=send_z.at[d - 1],
            recv_sem=recv_z.at[d - 1],
            device_id=ahead[d - 1],
            device_id_type=MESH,
        )
        copy.start()
        copies.append(copy)
    total = whole[tile].astype(F32)
    for d in range(1, tiles):
        copies[d - 1].wait()
        total = total + last[d - 1].astype(F32)
    total = total.astype(BF16).astype(F32)
    block[...] = jnp.zeros_like(block)
    for c in range(total.shape[0]):
        for z in range(CZ):
            block[z, :, c, :] = total[c, z * YT : (z + 1) * YT]
    exchange(block, padded, 2, send_h, recv_h)


def reduce_field(field):
    slabs, tiles, attrs, size, lanes = field.shape
    bits = slabs.bit_length() - 1
    half = tiles // 2
    parts = []
    for stage in range(bits):
        shape = (2,) * (bits - 1 - stage) + (half, attrs, size, lanes)
        parts += [pltpu.VMEM(shape, BF16)] * 2
    scratch = parts + parts
    scratch += [
        pltpu.VMEM((tiles - 1, attrs, size, lanes), BF16),
        pltpu.VMEM((CZ, YT, 8, lanes), F32),
        pltpu.SemaphoreType.DMA((2 * bits,)),
        pltpu.SemaphoreType.DMA((2 * bits,)),
        pltpu.SemaphoreType.DMA((tiles - 1,)),
        pltpu.SemaphoreType.DMA((tiles - 1,)),
        pltpu.SemaphoreType.DMA((8,)),
        pltpu.SemaphoreType.DMA((8,)),
        pltpu.VMEM((tiles, attrs, size, lanes), BF16),
    ]
    return pl.pallas_call(
        functools.partial(reduce_kernel, bits),
        in_specs=[pl.BlockSpec(memory_space=pltpu.VMEM)],
        out_specs=pl.BlockSpec(memory_space=pltpu.VMEM),
        out_shape=jax.ShapeDtypeStruct((CZ + 4, YT + 4, 8, lanes), F32),
        scratch_shapes=scratch,
        compiler_params=pltpu.CompilerParams(
            collective_id=0, has_side_effects=True, vmem_limit_bytes=56 << 20
        ),
        name="reduce_field",
    )(field.reshape((2,) * bits + field.shape[1:]))


def spread(values):
    return jnp.concatenate(
        [pltpu.roll(values, 1, 1), values, pltpu.roll(values, NX - 1, 1)], 0
    ).astype(BF16)


def conv_rows(stack, weight, acc):
    planes, rows = stack.shape[0] - 2, stack.shape[1] - 2
    outs = weight.shape[2]
    lefts = [jnp.concatenate([weight[a, b] for a in range(3)], 0) for b in range(3)]
    for z in range(planes + 2):
        for j in range(rows // 2):
            part = None
            for b in range(3):
                y = 2 * j + b
                pair = jnp.concatenate([stack[z, y], stack[z, y + 1]], 1)
                term = dot(lefts[b], pair)
                part = term if part is None else part + term
            for a in range(3):
                if 0 <= z - a < planes:
                    piece = part[a * outs : (a + 1) * outs]
                    if a == 0:
                        acc[z, j] = piece
                    else:
                        acc[z - a, j] += piece


def lane_index(rows):
    return lax.broadcasted_iota(jnp.int32, (rows, 128), 1)


def fine_kernel(grid, lift, fine, down, second, lowered, wide, stack, acc):
    planes, rows = grid.shape[0] - 2, grid.shape[1] - 2
    for z in range(planes + 2):
        block = grid[z]
        wide[z, :, 0:8] = pltpu.roll(block, 1, 2)
        wide[z, :, 8:16] = block
        wide[z, :, 16:24] = pltpu.roll(block, NX - 1, 2)

    def lift_plane(z, carry):
        for y in range(0, rows, 2):
            pair = jnp.concatenate(
                [
                    jnp.concatenate(
                        [wide[z + a, y + s + b] for a in range(3) for b in range(3)], 0
                    ).astype(BF16)
                    for s in range(2)
                ],
                1,
            )
            values = act(dot(lift[...], pair))
            stack[z, y] = spread(values[:, :NX])
            stack[z, y + 1] = spread(values[:, NX:])
        return carry

    lax.fori_loop(0, planes, lift_plane, 0)
    conv_rows(stack, fine, acc)
    for z in range(CZ):
        for j in range(YT // 2):
            values = act(acc[z, j]).astype(BF16)
            second[z, 2 * j] = values[:, :NX]
            second[z, 2 * j + 1] = values[:, NX:]
    source = lax.broadcasted_iota(jnp.int32, (NX, NX), 0)
    target = lax.broadcasted_iota(jnp.int32, (NX, NX), 1)
    half = NX // 2
    parity = jnp.where(target < half, 0, 1)
    sel = jnp.where(source == 2 * (target - half * parity) + parity, 1.0, 0.0).astype(BF16)
    chans = down.shape[0] // 2
    lane = lane_index(chans // 2)
    for z in range(CZ // 2):
        for j in range(YT // 4):
            pair = []
            for y in (2 * j, 2 * j + 1):
                tall = jnp.concatenate(
                    [second[2 * z + a, 2 * y + b] for a in range(2) for b in range(2)], 0
                )
                pair.append(dot(tall, sel).astype(BF16))
            out = dot(down[...], jnp.concatenate(pair, 1))
            for s in range(2):
                q = out[:, s * NX : (s + 1) * NX]
                h = chans // 2
                q00, q01, q10, q11 = (q[i * h : (i + 1) * h] for i in range(4))
                row = jnp.where(lane < half, q00, q11) + pltpu.roll(
                    jnp.where(lane < half, q01, q10), half, 1
                )
                lowered[z, 2 * j + s] = act(row).astype(BF16)


def fine_level(grid, lift, fine, down):
    outs, chans = fine.shape[2], down.shape[3]
    planes, rows = grid.shape[0] - 2, grid.shape[1] - 2
    wide = lift.reshape(3, 3, outs, 3, -1)
    wide = jnp.pad(wide, ((0, 0),) * 4 + ((0, 8 - wide.shape[4]),))
    wide = wide.transpose(2, 0, 1, 3, 4).reshape(outs, -1)
    low = down.transpose(2, 3, 0, 1, 4).reshape(2 * chans, 4 * outs)
    return pl.pallas_call(
        fine_kernel,
        out_shape=(
            jax.ShapeDtypeStruct((CZ, YT, outs, NX), BF16),
            jax.ShapeDtypeStruct((CZ // 2, YT // 2, chans // 2, NX), BF16),
        ),
        scratch_shapes=[
            pltpu.VMEM((planes + 2, rows + 2, 24, NX), F32),
            pltpu.VMEM((planes, rows, 3 * outs, NX), BF16),
            pltpu.VMEM((CZ, YT // 2, outs, 2 * NX), F32),
        ],
        compiler_params=pltpu.CompilerParams(vmem_limit_bytes=48 << 20),
        name="fine_level",
    )(grid, wide, fine, low)


def coarse_kernel(low, weight, up, second, joined, acc):
    half = NX // 2
    chans = weight.shape[2]
    outs = up.shape[3]
    lane = lane_index(chans // 2)
    planes = low.shape[0]
    for z in range(planes):
        row = [low[z, y].astype(F32) for y in range(low.shape[1])]
        turned = [pltpu.roll(r, half, 1) for r in row]
        pairs = []
        for r in range(len(row) - 1):
            top = jnp.where(lane < half, row[r], turned[r + 1])
            bottom = jnp.where(lane < half, turned[r], row[r + 1])
            pairs.append(jnp.concatenate([top, bottom], 0).astype(BF16))
        for b in range(3):
            right = jnp.concatenate([pairs[b], pairs[2 + b]], 1)
            for a in range(3):
                if 0 <= z - a < planes - 2:
                    for k in range(3):
                        part = dot(weight[a, b, :, k * chans : (k + 1) * chans], right)
                        if a == 0 and b == 0:
                            acc[z - a, k] = part
                        else:
                            acc[z - a, k] += part
    source = lax.broadcasted_iota(jnp.int32, (NX, 4 * NX), 0)
    target = lax.broadcasted_iota(jnp.int32, (NX, 4 * NX), 1)
    spot = target % NX
    want = target // (2 * NX) * half + spot // 2
    sel = jnp.where((source == want) & (spot % 2 == target // NX % 2), 1.0, 0.0).astype(BF16)
    lane = lane_index(chans)
    lefts = [
        jnp.concatenate([up[a, b, k] for a in range(2) for b in range(2)], 0) for k in range(2)
    ]
    for z in range(planes - 2):
        for j in range(2):
            at = slice(j * NX, (j + 1) * NX)
            before, same, after = (acc[z, k, :, at] for k in range(3))
            before = jnp.where(
                lane % half == 0, pltpu.roll(before, half + 1, 1), pltpu.roll(before, 1, 1)
            )
            after = jnp.where(
                lane % half == half - 1,
                pltpu.roll(after, half - 1, 1),
                pltpu.roll(after, NX - 1, 1),
            )
            coarse = act(before + same + after).astype(BF16)
            wide = dot(coarse, sel).astype(BF16)
            right = [
                jnp.concatenate([wide[:, k * NX : (k + 1) * NX], wide[:, (2 + k) * NX : (3 + k) * NX]], 1)
                for k in range(2)
            ]
            raised = dot(lefts[0], right[0]) + dot(lefts[1], right[1])
            for a in range(2):
                for b in range(2):
                    for p in range(2):
                        y = 2 * (2 * j + p) + b
                        piece = raised[
                            (2 * a + b) * outs : (2 * a + b + 1) * outs, p * NX : (p + 1) * NX
                        ]
                        joined[2 * z + a, y] = (second[2 * z + a, y].astype(F32) + piece).astype(
                            BF16
                        )


def coarse_level(low, weight, up, second):
    chans = weight.shape[2]
    return pl.pallas_call(
        coarse_kernel,
        out_shape=jax.ShapeDtypeStruct(second.shape, BF16),
        scratch_shapes=[pltpu.VMEM((CZ // 2, 3, chans, 2 * NX), F32)],
        compiler_params=pltpu.CompilerParams(vmem_limit_bytes=48 << 20),
        name="coarse_level",
    )(low, weight, up, second)


def merge_kernel(joined, weight, head, out, stack, acc):
    planes, rows = joined.shape[:2]

    def widen(z, carry):
        for y in range(rows):
            stack[z, y] = spread(joined[z, y].astype(F32))
        return carry

    lax.fori_loop(0, planes, widen, 0)
    conv_rows(stack, weight, acc)
    for z in range(planes - 2):
        for j in range(rows // 2 - 1):
            moved = dot(head[...], act(acc[z, j]).astype(BF16))
            for s in range(2):
                out[:, z, 2 * j + s, :] = moved[: out.shape[0], s * NX : (s + 1) * NX]


def merge_level(joined, weight, head):
    planes, rows, chans, lanes = joined.shape
    final = head.shape[0]
    padded = jnp.pad(head, ((0, 16 - final), (0, 0)))
    return pl.pallas_call(
        merge_kernel,
        out_shape=jax.ShapeDtypeStruct((final, planes - 2, rows - 2, lanes), F32),
        scratch_shapes=[
            pltpu.VMEM((planes, rows, 3 * chans, lanes), BF16),
            pltpu.VMEM((planes - 2, rows // 2 - 1, chans, 2 * lanes), F32),
        ],
        compiler_params=pltpu.CompilerParams(vmem_limit_bytes=48 << 20),
        name="merge_level",
    )(joined, weight, padded)


GROUP = 4
CHUNK = 512


def deposit_kernel(slabs, tiles, feat_ref, dest_ref, cell_ref, code_ref, live_ref, out_ref, right, acc):
    group = pl.program_id(0)
    rows = feat_ref.shape[1]
    attrs = feat_ref.shape[0]
    ny = tiles * YT
    nz = slabs * CZ
    f32 = jnp.float32

    @pl.when(group == 0)
    def _():
        def build(j, carry):
            at = pl.ds(pl.multiple_of(j * CHUNK, CHUNK), CHUNK)
            cells = cell_ref[:, at]
            codes = code_ref[:, at]
            lane = lax.broadcasted_iota(jnp.int32, (1, CHUNK), 1) + j * CHUNK
            live = lane < live_ref[0]
            feats = jnp.where(live, feat_ref[:, at].astype(f32), 0.0)
            frac = (codes & 63).astype(f32) * (1.0 / 64.0)
            col = cells & (NX - 1)
            nxt = (col + 1) & (NX - 1)
            xs = lax.broadcasted_iota(jnp.int32, (NX, CHUNK), 0)
            wx = jnp.where(xs == col, 1.0 - frac, 0.0) + jnp.where(xs == nxt, frac, 0.0)
            for c in range(attrs):
                right[c * NX : (c + 1) * NX, at] = (wx * feats[c : c + 1, :]).astype(jnp.bfloat16)
            return carry

        lax.fori_loop(0, rows // CHUNK, build, 0)

    def step(j, carry):
        at = pl.ds(pl.multiple_of(j * CHUNK, CHUNK), CHUNK)
        cells = cell_ref[:, at]
        codes = code_ref[:, at]
        fz = ((codes >> 12) & 63).astype(f32) * (1.0 / 64.0)
        fy = ((codes >> 6) & 63).astype(f32) * (1.0 / 64.0)
        row = cells // NX
        y0 = row % ny
        z0 = dest_ref[:, at] * CZ + row // ny
        y1 = (y0 + 1) % ny
        z1 = (z0 + 1) % nz
        ys = lax.broadcasted_iota(jnp.int32, (ny, CHUNK), 0)
        wy = jnp.where(ys == y0, 1.0 - fy, 0.0) + jnp.where(ys == y1, fy, 0.0)
        zs = lax.broadcasted_iota(jnp.int32, (GROUP * CZ, CHUNK), 0) + group * GROUP * CZ
        wz = jnp.where(zs == z0, 1.0 - fz, 0.0) + jnp.where(zs == z1, fz, 0.0)
        pieces = []
        for s in range(GROUP):
            for t in range(tiles):
                for z in range(CZ):
                    k = s * CZ + z
                    pieces.append(wz[k : k + 1, :] * wy[t * YT : (t + 1) * YT, :])
        left = jnp.concatenate(pieces, 0).astype(jnp.bfloat16)
        part = lax.dot_general(
            left, right[:, at], (((1,), (1,)), ((), ())), preferred_element_type=f32
        )

        @pl.when(j == 0)
        def _():
            acc[...] = part

        @pl.when(j > 0)
        def _():
            acc[...] += part

        return carry

    lax.fori_loop(0, rows // CHUNK, step, 0)
    size = CZ * YT
    for s in range(GROUP):
        for t in range(tiles):
            k = (s * tiles + t) * size
            for c in range(attrs):
                out_ref[s, t, c] = acc[k : k + size, c * NX : (c + 1) * NX].astype(jnp.bfloat16)


def deposit(features, destination, cell_index, offset_code, live_count, slabs, tiles):
    attrs, rows = features.shape
    size = CZ * YT
    whole = lambda shape: pl.BlockSpec(shape, lambda g: (0, 0))
    return pl.pallas_call(
        functools.partial(deposit_kernel, slabs, tiles),
        grid=(slabs // GROUP,),
        in_specs=[
            whole((attrs, rows)),
            whole((1, rows)),
            whole((1, rows)),
            whole((1, rows)),
            pl.BlockSpec(memory_space=pltpu.SMEM),
        ],
        out_specs=pl.BlockSpec((GROUP, tiles, attrs, size, NX), lambda g: (g, 0, 0, 0, 0)),
        out_shape=jax.ShapeDtypeStruct((slabs, tiles, attrs, size, NX), jnp.bfloat16),
        scratch_shapes=[
            pltpu.VMEM((attrs * NX, rows), jnp.bfloat16),
            pltpu.VMEM((GROUP * tiles * size, attrs * NX), jnp.float32),
        ],
        compiler_params=pltpu.CompilerParams(vmem_limit_bytes=48 << 20),
        name="deposit",
    )(
        features,
        destination.reshape(1, rows),
        cell_index.reshape(1, rows),
        offset_code.reshape(1, rows),
        live_count,
    )


def body(
    particle_features,
    destination,
    cell_index,
    offset_code,
    live_count,
    lift_weight,
    fine_weight,
    down_weight,
    coarse_weight,
    up_weight,
    merge_weight,
    head_weight,
):
    slabs = lax.axis_size("slab")
    tiles = lax.axis_size("tile")
    field = deposit(
        particle_features, destination, cell_index, offset_code, live_count, slabs, tiles
    )
    grid = reduce_field(field)
    second, lowered = fine_level(grid, lift_weight, fine_weight, down_weight)
    lowered = with_halo(lowered, 1, 1)
    joined = coarse_level(lowered, coarse_weight, up_weight, second)
    joined = with_halo(joined, 1, 2)
    return merge_level(joined, merge_weight, head_weight)


def solution(mesh):
    placed = (
        P(None, ("slab", "tile")),
        P(("slab", "tile"), None),
        P(("slab", "tile")),
        P(("slab", "tile")),
        P(("slab", "tile")),
        P(),
        P(),
        P(),
        P(),
        P(),
        P(),
        P(),
    )
    return jax.shard_map(
        body, mesh=mesh, in_specs=placed, out_specs=P(None, "slab", "tile", None), check_vma=False
    )
```

```python
import functools

import jax
import jax.numpy as jnp
from jax import lax
from jax.experimental import pallas as pl
from jax.experimental.pallas import tpu as pltpu
from jax.sharding import PartitionSpec as P

NX = 128
YT = 8
CZ = 4


slope = 0.1


BF16 = jnp.bfloat16
F32 = jnp.float32
MESH = pl.DeviceIdType.MESH
SIDES = [(dz, dy) for dz in (-1, 0, 1) for dy in (-1, 0, 1) if dz or dy]


def act(values):
    return jnp.maximum(values, slope * values)


def dot(left, right):
    return jnp.dot(left, right, preferred_element_type=F32)


def neighbour(dz, dy):
    slabs, tiles = lax.axis_size("slab"), lax.axis_size("tile")
    return (
        lax.rem(lax.axis_index("slab") + (dz + slabs), slabs),
        lax.rem(lax.axis_index("tile") + (dy + tiles), tiles),
    )


def greet(devices):
    barrier = pltpu.get_barrier_semaphore()
    for device in devices:
        pl.semaphore_signal(barrier, inc=1, device_id=device, device_id_type=MESH)
    pl.semaphore_wait(barrier, len(devices))


def span(shift, size, width):
    if shift > 0:
        return pl.ds(size - width, width), pl.ds(0, width)
    if shift < 0:
        return pl.ds(0, width), pl.ds(size + width, width)
    return pl.ds(0, size), pl.ds(width, size)


def exchange(block, padded, width, send, recv):
    planes, rows = block.shape[:2]
    copies = []
    for n, (dz, dy) in enumerate(SIDES):
        from_z, to_z = span(dz, planes, width)
        from_y, to_y = span(dy, rows, width)
        copies.append(
            pltpu.make_async_remote_copy(
                src_ref=block.at[from_z, from_y],
                dst_ref=padded.at[to_z, to_y],
                send_sem=send.at[n],
                recv_sem=recv.at[n],
                device_id=neighbour(dz, dy),
                device_id_type=MESH,
            )
        )
    for copy in copies:
        copy.start()
    padded[pl.ds(width, planes), pl.ds(width, rows)] = block[...]
    for copy in copies:
        copy.wait()


def halo_kernel(width, block, padded, send, recv):
    greet([neighbour(dz, dy) for dz, dy in SIDES])
    exchange(block, padded, width, send, recv)


def with_halo(block, width, number):
    planes, rows, depth, lanes = block.shape
    return pl.pallas_call(
        functools.partial(halo_kernel, width),
        in_specs=[pl.BlockSpec(memory_space=pltpu.VMEM)],
        out_specs=pl.BlockSpec(memory_space=pltpu.VMEM),
        out_shape=jax.ShapeDtypeStruct(
            (planes + 2 * width, rows + 2 * width, depth, lanes), block.dtype
        ),
        scratch_shapes=[pltpu.SemaphoreType.DMA((8,)), pltpu.SemaphoreType.DMA((8,))],
        compiler_params=pltpu.CompilerParams(
            collective_id=number, has_side_effects=True, vmem_limit_bytes=32 << 20
        ),
        name=f"halo{number}",
    )(block)


def reduce_kernel(bits, field, padded, *scratch):
    tiles = lax.axis_size("tile")
    attrs = field.shape[0]
    slab, tile = lax.axis_index("slab"), lax.axis_index("tile")
    mine = [slab // 2**b % 2 for b in range(bits)]
    partner = [(slab + 2**b * (1 - 2 * mine[b]), tile) for b in range(bits)]
    ahead = [(slab, lax.rem(tile + d, tiles)) for d in range(1, tiles)]
    greet(partner + ahead + [neighbour(dz, dy) for dz, dy in SIDES])
    gets, sums = scratch[:bits], scratch[bits : 2 * bits]
    last, block, send, recv, send_z, recv_z, send_h, recv_h = scratch[2 * bits :]
    orders = [[0] + list(range(1, bits)), [0] + list(range(bits - 1, 0, -1))]

    def part(c, stage, side):
        order = orders[c % 2]
        rest = [b for b in range(bits - 1, -1, -1) if b not in order[:stage]]
        b = order[stage]
        source = field if stage == 0 else sums[stage - 1]
        which = mine[b] if side == 0 else 1 - mine[b]
        return source, (c,) + (slice(None),) * rest.index(b) + (which,)

    def push(c, stage):
        source, at = part(c, stage, 1)
        copy = pltpu.make_async_remote_copy(
            src_ref=source.at[at],
            dst_ref=gets[stage].at[c],
            send_sem=send.at[stage, c],
            recv_sem=recv.at[stage, c],
            device_id=partner[orders[c % 2][stage]],
            device_id_type=MESH,
        )
        copy.start()
        return copy

    def deal(c):
        copies = []
        for d in range(1, tiles):
            copy = pltpu.make_async_remote_copy(
                src_ref=sums[bits - 1].at[c, lax.rem(tile + d, tiles)],
                dst_ref=last.at[c, d - 1],
                send_sem=send_z.at[c, d - 1],
                recv_sem=recv_z.at[c, d - 1],
                device_id=ahead[d - 1],
                device_id_type=MESH,
            )
            copy.start()
            copies.append(copy)
        return copies

    flying = [push(c, 0) for c in range(attrs)]
    for stage in range(bits):
        for c in range(attrs):
            flying[c].wait()
            source, at = part(c, stage, 0)
            total = source[at].astype(F32) + gets[stage][c].astype(F32)
            sums[stage][c] = total.astype(BF16)
            flying[c] = push(c, stage + 1) if stage < bits - 1 else deal(c)
    block[...] = jnp.zeros_like(block)
    for c in range(attrs):
        total = sums[bits - 1][c, tile].astype(F32)
        for d in range(1, tiles):
            flying[c][d - 1].wait()
            total = total + last[c, d - 1].astype(F32)
        total = total.astype(BF16).astype(F32)
        for z in range(CZ):
            block[z, :, c, :] = total[z * YT : (z + 1) * YT]
    exchange(block, padded, 2, send_h, recv_h)


def reduce_field(field):
    attrs, slabs, tiles, size, lanes = field.shape
    bits = slabs.bit_length() - 1
    parts = [
        pltpu.VMEM((attrs,) + (2,) * (bits - 1 - stage) + (tiles, size, lanes), BF16)
        for stage in range(bits)
    ]
    scratch = parts + parts
    scratch += [
        pltpu.VMEM((attrs, tiles - 1, size, lanes), BF16),
        pltpu.VMEM((CZ, YT, 8, lanes), F32),
        pltpu.SemaphoreType.DMA((bits, attrs)),
        pltpu.SemaphoreType.DMA((bits, attrs)),
        pltpu.SemaphoreType.DMA((attrs, tiles - 1)),
        pltpu.SemaphoreType.DMA((attrs, tiles - 1)),
        pltpu.SemaphoreType.DMA((8,)),
        pltpu.SemaphoreType.DMA((8,)),
    ]
    return pl.pallas_call(
        functools.partial(reduce_kernel, bits),
        in_specs=[pl.BlockSpec(memory_space=pltpu.VMEM)],
        out_specs=pl.BlockSpec(memory_space=pltpu.VMEM),
        out_shape=jax.ShapeDtypeStruct((CZ + 4, YT + 4, 8, lanes), F32),
        scratch_shapes=scratch,
        compiler_params=pltpu.CompilerParams(
            collective_id=0, has_side_effects=True, vmem_limit_bytes=56 << 20
        ),
        name="reduce_field",
    )(field.reshape((attrs,) + (2,) * bits + field.shape[2:]))


def spread(values):
    return jnp.concatenate(
        [pltpu.roll(values, 1, 1), values, pltpu.roll(values, NX - 1, 1)], 0
    ).astype(BF16)


def conv_rows(stack, weight, acc):
    planes, rows = stack.shape[0] - 2, stack.shape[1] - 2
    outs = weight.shape[2]
    lefts = [jnp.concatenate([weight[a, b] for a in range(3)], 0) for b in range(3)]
    for z in range(planes + 2):
        for j in range(rows // 2):
            part = None
            for b in range(3):
                y = 2 * j + b
                pair = jnp.concatenate([stack[z, y], stack[z, y + 1]], 1)
                term = dot(lefts[b], pair)
                part = term if part is None else part + term
            for a in range(3):
                if 0 <= z - a < planes:
                    piece = part[a * outs : (a + 1) * outs]
                    if a == 0:
                        acc[z, j] = piece
                    else:
                        acc[z - a, j] += piece


def lane_index(rows):
    return lax.broadcasted_iota(jnp.int32, (rows, 128), 1)


def place(rows, columns, target_of):
    source = lax.broadcasted_iota(jnp.int32, (rows, columns), 0)
    target = lax.broadcasted_iota(jnp.int32, (rows, columns), 1)
    return jnp.where(target == target_of(source), 1.0, 0.0).astype(BF16)


def fine_kernel(grid, lift_raw, fine, down_raw, second, lowered, wide, stack, acc, lift, down):
    planes, rows = grid.shape[0] - 2, grid.shape[1] - 2
    taps = lift_raw.shape[3]
    each = taps // 3
    total = None
    for n in range(9):
        spots = place(taps, 216, lambda i: n * 24 + i // each * 8 + i % each)
        term = dot(lift_raw[n // 3, n % 3], spots)
        total = term if total is None else total + term
    lift[...] = total.astype(BF16)
    depth = down_raw.shape[2]
    total = None
    for n in range(4):
        term = dot(down_raw[n], place(depth, 4 * depth, lambda i: n * depth + i))
        total = term if total is None else total + term
    down[...] = total.astype(BF16)
    for z in range(planes + 2):
        block = grid[z]
        wide[z, :, 0:8] = pltpu.roll(block, 1, 2)
        wide[z, :, 8:16] = block
        wide[z, :, 16:24] = pltpu.roll(block, NX - 1, 2)

    def lift_plane(z, carry):
        for y in range(0, rows, 2):
            pair = jnp.concatenate(
                [
                    jnp.concatenate(
                        [wide[z + a, y + s + b] for a in range(3) for b in range(3)], 0
                    ).astype(BF16)
                    for s in range(2)
                ],
                1,
            )
            values = act(dot(lift[...], pair))
            stack[z, y] = spread(values[:, :NX])
            stack[z, y + 1] = spread(values[:, NX:])
        return carry

    lax.fori_loop(0, planes, lift_plane, 0)
    conv_rows(stack, fine, acc)
    for z in range(CZ):
        for j in range(YT // 2):
            values = act(acc[z, j]).astype(BF16)
            second[z, 2 * j] = values[:, :NX]
            second[z, 2 * j + 1] = values[:, NX:]
    source = lax.broadcasted_iota(jnp.int32, (NX, NX), 0)
    target = lax.broadcasted_iota(jnp.int32, (NX, NX), 1)
    half = NX // 2
    parity = jnp.where(target < half, 0, 1)
    sel = jnp.where(source == 2 * (target - half * parity) + parity, 1.0, 0.0).astype(BF16)
    chans = down.shape[0] // 2
    lane = lane_index(chans // 2)
    for z in range(CZ // 2):
        for j in range(YT // 4):
            pair = []
            for y in (2 * j, 2 * j + 1):
                tall = jnp.concatenate(
                    [second[2 * z + a, 2 * y + b] for a in range(2) for b in range(2)], 0
                )
                pair.append(dot(tall, sel).astype(BF16))
            out = dot(down[...], jnp.concatenate(pair, 1))
            for s in range(2):
                q = out[:, s * NX : (s + 1) * NX]
                h = chans // 2
                q00, q01, q10, q11 = (q[i * h : (i + 1) * h] for i in range(4))
                row = jnp.where(lane < half, q00, q11) + pltpu.roll(
                    jnp.where(lane < half, q01, q10), half, 1
                )
                lowered[z, 2 * j + s] = act(row).astype(BF16)


def fine_level(grid, lift, fine, down):
    outs, chans = fine.shape[2], down.shape[3]
    planes, rows = grid.shape[0] - 2, grid.shape[1] - 2
    low = down.reshape(4, 2 * chans, outs)
    return pl.pallas_call(
        fine_kernel,
        out_shape=(
            jax.ShapeDtypeStruct((CZ, YT, outs, NX), BF16),
            jax.ShapeDtypeStruct((CZ // 2, YT // 2, chans // 2, NX), BF16),
        ),
        scratch_shapes=[
            pltpu.VMEM((planes + 2, rows + 2, 24, NX), F32),
            pltpu.VMEM((planes, rows, 3 * outs, NX), BF16),
            pltpu.VMEM((CZ, YT // 2, outs, 2 * NX), F32),
            pltpu.VMEM((outs, 216), BF16),
            pltpu.VMEM((2 * chans, 4 * outs), BF16),
        ],
        compiler_params=pltpu.CompilerParams(vmem_limit_bytes=48 << 20),
        name="fine_level",
    )(grid, lift, fine, low)


def coarse_kernel(low, weight, up, second, joined, acc):
    half = NX // 2
    chans = weight.shape[2]
    outs = up.shape[3]
    lane = lane_index(chans // 2)
    planes = low.shape[0]
    for z in range(planes):
        row = [low[z, y].astype(F32) for y in range(low.shape[1])]
        turned = [pltpu.roll(r, half, 1) for r in row]
        pairs = []
        for r in range(len(row) - 1):
            top = jnp.where(lane < half, row[r], turned[r + 1])
            bottom = jnp.where(lane < half, turned[r], row[r + 1])
            pairs.append(jnp.concatenate([top, bottom], 0).astype(BF16))
        for b in range(3):
            right = jnp.concatenate([pairs[b], pairs[2 + b]], 1)
            for a in range(3):
                if 0 <= z - a < planes - 2:
                    for k in range(3):
                        part = dot(weight[a, b, :, k * chans : (k + 1) * chans], right)
                        if a == 0 and b == 0:
                            acc[z - a, k] = part
                        else:
                            acc[z - a, k] += part
    source = lax.broadcasted_iota(jnp.int32, (NX, 4 * NX), 0)
    target = lax.broadcasted_iota(jnp.int32, (NX, 4 * NX), 1)
    spot = target % NX
    want = target // (2 * NX) * half + spot // 2
    sel = jnp.where((source == want) & (spot % 2 == target // NX % 2), 1.0, 0.0).astype(BF16)
    lane = lane_index(chans)
    lefts = [
        jnp.concatenate([up[a, b, k] for a in range(2) for b in range(2)], 0) for k in range(2)
    ]
    for z in range(planes - 2):
        for j in range(2):
            at = slice(j * NX, (j + 1) * NX)
            before, same, after = (acc[z, k, :, at] for k in range(3))
            before = jnp.where(
                lane % half == 0, pltpu.roll(before, half + 1, 1), pltpu.roll(before, 1, 1)
            )
            after = jnp.where(
                lane % half == half - 1,
                pltpu.roll(after, half - 1, 1),
                pltpu.roll(after, NX - 1, 1),
            )
            coarse = act(before + same + after).astype(BF16)
            wide = dot(coarse, sel).astype(BF16)
            right = [
                jnp.concatenate([wide[:, k * NX : (k + 1) * NX], wide[:, (2 + k) * NX : (3 + k) * NX]], 1)
                for k in range(2)
            ]
            raised = dot(lefts[0], right[0]) + dot(lefts[1], right[1])
            for a in range(2):
                for b in range(2):
                    for p in range(2):
                        y = 2 * (2 * j + p) + b
                        piece = raised[
                            (2 * a + b) * outs : (2 * a + b + 1) * outs, p * NX : (p + 1) * NX
                        ]
                        joined[2 * z + a, y] = (second[2 * z + a, y].astype(F32) + piece).astype(
                            BF16
                        )


def coarse_level(low, weight, up, second):
    chans = weight.shape[2]
    return pl.pallas_call(
        coarse_kernel,
        out_shape=jax.ShapeDtypeStruct(second.shape, BF16),
        scratch_shapes=[pltpu.VMEM((CZ // 2, 3, chans, 2 * NX), F32)],
        compiler_params=pltpu.CompilerParams(vmem_limit_bytes=48 << 20),
        name="coarse_level",
    )(low, weight, up, second)


def merge_kernel(joined, weight, head, out, stack, acc):
    planes, rows = joined.shape[:2]

    def widen(z, carry):
        for y in range(rows):
            stack[z, y] = spread(joined[z, y].astype(F32))
        return carry

    lax.fori_loop(0, planes, widen, 0)
    conv_rows(stack, weight, acc)
    for z in range(planes - 2):
        for j in range(rows // 2 - 1):
            moved = dot(head[...], act(acc[z, j]).astype(BF16))
            for s in range(2):
                out[:, z, 2 * j + s, :] = moved[: out.shape[0], s * NX : (s + 1) * NX]


def merge_level(joined, weight, head):
    planes, rows, chans, lanes = joined.shape
    final = head.shape[0]
    return pl.pallas_call(
        merge_kernel,
        out_shape=jax.ShapeDtypeStruct((final, planes - 2, rows - 2, lanes), F32),
        scratch_shapes=[
            pltpu.VMEM((planes, rows, 3 * chans, lanes), BF16),
            pltpu.VMEM((planes - 2, rows // 2 - 1, chans, 2 * lanes), F32),
        ],
        compiler_params=pltpu.CompilerParams(vmem_limit_bytes=48 << 20),
        name="merge_level",
    )(joined, weight, head)


GROUP = 8
CHUNK = 512


def deposit_kernel(slabs, tiles, feat_ref, dest_ref, cell_ref, code_ref, live_ref, out_ref, right, acc):
    group = pl.program_id(0)
    rows = feat_ref.shape[1]
    attrs = feat_ref.shape[0]
    ny = tiles * YT
    nz = slabs * CZ
    f32 = jnp.float32

    @pl.when(group == 0)
    def _():
        def build(j, carry):
            at = pl.ds(pl.multiple_of(j * CHUNK, CHUNK), CHUNK)
            cells = cell_ref[:, at]
            codes = code_ref[:, at]
            lane = lax.broadcasted_iota(jnp.int32, (1, CHUNK), 1) + j * CHUNK
            live = lane < live_ref[0]
            feats = jnp.where(live, feat_ref[:, at].astype(f32), 0.0)
            frac = (codes & 63).astype(f32) * (1.0 / 64.0)
            col = cells & (NX - 1)
            nxt = (col + 1) & (NX - 1)
            xs = lax.broadcasted_iota(jnp.int32, (NX, CHUNK), 0)
            wx = jnp.where(xs == col, 1.0 - frac, 0.0) + jnp.where(xs == nxt, frac, 0.0)
            for c in range(attrs):
                right[c * NX : (c + 1) * NX, at] = (wx * feats[c : c + 1, :]).astype(jnp.bfloat16)
            return carry

        lax.fori_loop(0, rows // CHUNK, build, 0)

    def step(j, carry):
        at = pl.ds(pl.multiple_of(j * CHUNK, CHUNK), CHUNK)
        cells = cell_ref[:, at]
        codes = code_ref[:, at]
        fz = ((codes >> 12) & 63).astype(f32) * (1.0 / 64.0)
        fy = ((codes >> 6) & 63).astype(f32) * (1.0 / 64.0)
        row = cells // NX
        y0 = row % ny
        z0 = dest_ref[:, at] * CZ + row // ny
        y1 = (y0 + 1) % ny
        z1 = (z0 + 1) % nz
        ys = lax.broadcasted_iota(jnp.int32, (ny, CHUNK), 0)
        wy = jnp.where(ys == y0, 1.0 - fy, 0.0) + jnp.where(ys == y1, fy, 0.0)
        zs = lax.broadcasted_iota(jnp.int32, (GROUP * CZ, CHUNK), 0) + group * GROUP * CZ
        wz = jnp.where(zs == z0, 1.0 - fz, 0.0) + jnp.where(zs == z1, fz, 0.0)
        pieces = []
        for s in range(GROUP):
            for t in range(tiles):
                for z in range(CZ):
                    k = s * CZ + z
                    pieces.append(wz[k : k + 1, :] * wy[t * YT : (t + 1) * YT, :])
        left = jnp.concatenate(pieces, 0).astype(jnp.bfloat16)
        part = lax.dot_general(
            left, right[:, at], (((1,), (1,)), ((), ())), preferred_element_type=f32
        )

        @pl.when(j == 0)
        def _():
            acc[...] = part

        @pl.when(j > 0)
        def _():
            acc[...] += part

        return carry

    lax.fori_loop(0, rows // CHUNK, step, 0)
    size = CZ * YT
    for s in range(GROUP):
        for t in range(tiles):
            k = (s * tiles + t) * size
            for c in range(attrs):
                out_ref[c, s, t] = acc[k : k + size, c * NX : (c + 1) * NX].astype(jnp.bfloat16)


def deposit(features, destination, cell_index, offset_code, live_count, slabs, tiles):
    attrs, rows = features.shape
    size = CZ * YT
    whole = lambda shape: pl.BlockSpec(shape, lambda g: (0, 0))
    return pl.pallas_call(
        functools.partial(deposit_kernel, slabs, tiles),
        grid=(slabs // GROUP,),
        in_specs=[
            whole((attrs, rows)),
            whole((1, rows)),
            whole((1, rows)),
            whole((1, rows)),
            pl.BlockSpec(memory_space=pltpu.SMEM),
        ],
        out_specs=pl.BlockSpec((attrs, GROUP, tiles, size, NX), lambda g: (0, g, 0, 0, 0)),
        out_shape=jax.ShapeDtypeStruct((attrs, slabs, tiles, size, NX), jnp.bfloat16),
        scratch_shapes=[
            pltpu.VMEM((attrs * NX, rows), jnp.bfloat16),
            pltpu.VMEM((GROUP * tiles * size, attrs * NX), jnp.float32),
        ],
        compiler_params=pltpu.CompilerParams(vmem_limit_bytes=60 << 20),
        name="deposit",
    )(
        features,
        destination.reshape(1, rows),
        cell_index.reshape(1, rows),
        offset_code.reshape(1, rows),
        live_count,
    )


def body(
    particle_features,
    destination,
    cell_index,
    offset_code,
    live_count,
    lift_weight,
    fine_weight,
    down_weight,
    coarse_weight,
    up_weight,
    merge_weight,
    head_weight,
):
    slabs = lax.axis_size("slab")
    tiles = lax.axis_size("tile")
    field = deposit(
        particle_features, destination, cell_index, offset_code, live_count, slabs, tiles
    )
    grid = reduce_field(field)
    second, lowered = fine_level(grid, lift_weight, fine_weight, down_weight)
    lowered = with_halo(lowered, 1, 1)
    joined = coarse_level(lowered, coarse_weight, up_weight, second)
    joined = with_halo(joined, 1, 2)
    return merge_level(joined, merge_weight, head_weight)


def solution(mesh):
    placed = (
        P(None, ("slab", "tile")),
        P(("slab", "tile"), None),
        P(("slab", "tile")),
        P(("slab", "tile")),
        P(("slab", "tile")),
        P(),
        P(),
        P(),
        P(),
        P(),
        P(),
        P(),
    )
    return jax.shard_map(
        body, mesh=mesh, in_specs=placed, out_specs=P(None, "slab", "tile", None), check_vma=False
    )
```

```python
import functools

import jax
import jax.numpy as jnp
from jax import lax
from jax.experimental import pallas as pl
from jax.experimental.pallas import tpu as pltpu
from jax.sharding import PartitionSpec as P

NX = 128
YT = 8
CZ = 4


slope = 0.1


BF16 = jnp.bfloat16
F32 = jnp.float32
MESH = pl.DeviceIdType.MESH
SIDES = [(dz, dy) for dz in (-1, 0, 1) for dy in (-1, 0, 1) if dz or dy]


def act(values):
    return jnp.maximum(values, slope * values)


def dot(left, right):
    return jnp.dot(left, right, preferred_element_type=F32)


def neighbour(dz, dy):
    slabs, tiles = lax.axis_size("slab"), lax.axis_size("tile")
    return (
        lax.rem(lax.axis_index("slab") + (dz + slabs), slabs),
        lax.rem(lax.axis_index("tile") + (dy + tiles), tiles),
    )


def greet(devices):
    barrier = pltpu.get_barrier_semaphore()
    for device in devices:
        pl.semaphore_signal(barrier, inc=1, device_id=device, device_id_type=MESH)
    pl.semaphore_wait(barrier, len(devices))


def span(shift, size, width):
    if shift > 0:
        return pl.ds(size - width, width), pl.ds(0, width)
    if shift < 0:
        return pl.ds(0, width), pl.ds(size + width, width)
    return pl.ds(0, size), pl.ds(width, size)


def exchange(block, padded, width, send, recv):
    planes, rows = block.shape[:2]
    copies = []
    for n, (dz, dy) in enumerate(SIDES):
        from_z, to_z = span(dz, planes, width)
        from_y, to_y = span(dy, rows, width)
        copies.append(
            pltpu.make_async_remote_copy(
                src_ref=block.at[from_z, from_y],
                dst_ref=padded.at[to_z, to_y],
                send_sem=send.at[n],
                recv_sem=recv.at[n],
                device_id=neighbour(dz, dy),
                device_id_type=MESH,
            )
        )
    for copy in copies:
        copy.start()
    padded[pl.ds(width, planes), pl.ds(width, rows)] = block[...]
    for copy in copies:
        copy.wait()


def meet(bits):
    slab, tile, tiles = lax.axis_index("slab"), lax.axis_index("tile"), lax.axis_size("tile")
    partner = [(slab + 2**b * (1 - 2 * (slab // 2**b % 2)), tile) for b in range(bits)]
    ahead = [(slab, lax.rem(tile + d, tiles)) for d in range(1, tiles)]
    greet(partner + ahead + [neighbour(dz, dy) for dz, dy in SIDES])


def reduce_stage(bits, field, padded, *scratch):
    tiles = lax.axis_size("tile")
    attrs = field.shape[0]
    slab, tile = lax.axis_index("slab"), lax.axis_index("tile")
    mine = [slab // 2**b % 2 for b in range(bits)]
    partner = [(slab + 2**b * (1 - 2 * mine[b]), tile) for b in range(bits)]
    ahead = [(slab, lax.rem(tile + d, tiles)) for d in range(1, tiles)]
    gets, sums = scratch[:bits], scratch[bits : 2 * bits]
    last, block, send, recv, send_z, recv_z, send_h, recv_h = scratch[2 * bits :]
    orders = [[0] + list(range(1, bits)), [0] + list(range(bits - 1, 0, -1))]

    def part(c, stage, side):
        order = orders[c % 2]
        rest = [b for b in range(bits - 1, -1, -1) if b not in order[:stage]]
        b = order[stage]
        source = field if stage == 0 else sums[stage - 1]
        which = mine[b] if side == 0 else 1 - mine[b]
        return source, (c,) + (slice(None),) * rest.index(b) + (which,)

    def push(c, stage):
        source, at = part(c, stage, 1)
        copy = pltpu.make_async_remote_copy(
            src_ref=source.at[at],
            dst_ref=gets[stage].at[c],
            send_sem=send.at[stage, c],
            recv_sem=recv.at[stage, c],
            device_id=partner[orders[c % 2][stage]],
            device_id_type=MESH,
        )
        copy.start()
        return copy

    def deal(c):
        copies = []
        for d in range(1, tiles):
            copy = pltpu.make_async_remote_copy(
                src_ref=sums[bits - 1].at[c, lax.rem(tile + d, tiles)],
                dst_ref=last.at[c, d - 1],
                send_sem=send_z.at[c, d - 1],
                recv_sem=recv_z.at[c, d - 1],
                device_id=ahead[d - 1],
                device_id_type=MESH,
            )
            copy.start()
            copies.append(copy)
        return copies

    flying = [push(c, 0) for c in range(attrs)]
    for stage in range(bits):
        for c in range(attrs):
            flying[c].wait()
            source, at = part(c, stage, 0)
            total = source[at].astype(F32) + gets[stage][c].astype(F32)
            sums[stage][c] = total.astype(BF16)
            flying[c] = push(c, stage + 1) if stage < bits - 1 else deal(c)
    block[...] = jnp.zeros_like(block)
    for c in range(attrs):
        total = sums[bits - 1][c, tile].astype(F32)
        for d in range(1, tiles):
            flying[c][d - 1].wait()
            total = total + last[c, d - 1].astype(F32)
        total = total.astype(BF16).astype(F32)
        for z in range(CZ):
            block[z, :, c, :] = total[z * YT : (z + 1) * YT]
    exchange(block, padded, 2, send_h, recv_h)


def spread(values):
    return jnp.concatenate(
        [pltpu.roll(values, 1, 1), values, pltpu.roll(values, NX - 1, 1)], 0
    ).astype(BF16)


def conv_rows(stack, weight, acc):
    planes, rows = stack.shape[0] - 2, stack.shape[1] - 2
    outs = weight.shape[2]
    lefts = [jnp.concatenate([weight[a, b] for a in range(3)], 0) for b in range(3)]
    for z in range(planes + 2):
        for j in range(rows // 2):
            part = None
            for b in range(3):
                y = 2 * j + b
                pair = jnp.concatenate([stack[z, y], stack[z, y + 1]], 1)
                term = dot(lefts[b], pair)
                part = term if part is None else part + term
            for a in range(3):
                if 0 <= z - a < planes:
                    piece = part[a * outs : (a + 1) * outs]
                    if a == 0:
                        acc[z, j] = piece
                    else:
                        acc[z - a, j] += piece


def lane_index(rows):
    return lax.broadcasted_iota(jnp.int32, (rows, 128), 1)


def cross(left, right):
    return lax.dot_general(left, right, (((0,), (0,)), ((), ())), preferred_element_type=F32)


def place(rows, columns, target_of):
    source = lax.broadcasted_iota(jnp.int32, (rows, columns), 0)
    target = lax.broadcasted_iota(jnp.int32, (rows, columns), 1)
    return jnp.where(target == target_of(source), 1.0, 0.0).astype(BF16)


def fine_kernel(grid, lift_raw, fine, down_raw, second, lowered, wide, stack, acc, lift, down):
    planes, rows = grid.shape[0] - 2, grid.shape[1] - 2
    taps = lift_raw.shape[2]
    each = taps // 3
    total = None
    for n in range(9):
        spots = place(taps, 216, lambda i: n * 24 + i // each * 8 + i % each)
        term = cross(lift_raw[n // 3, n % 3], spots)
        total = term if total is None else total + term
    lift[...] = total.astype(BF16)
    depth, tall = down_raw.shape[3:]
    for k in range(2):
        total = None
        for n in range(4):
            spots = place(depth, 4 * depth, lambda i: n * depth + i)
            term = cross(down_raw[n // 2, n % 2, k], spots)
            total = term if total is None else total + term
        down[k * tall : (k + 1) * tall] = total.astype(BF16)
    for z in range(planes + 2):
        block = grid[z]
        wide[z, :, 0:8] = pltpu.roll(block, 1, 2)
        wide[z, :, 8:16] = block
        wide[z, :, 16:24] = pltpu.roll(block, NX - 1, 2)

    def lift_plane(z, carry):
        for y in range(0, rows, 2):
            pair = jnp.concatenate(
                [
                    jnp.concatenate(
                        [wide[z + a, y + s + b] for a in range(3) for b in range(3)], 0
                    ).astype(BF16)
                    for s in range(2)
                ],
                1,
            )
            values = act(dot(lift[...], pair))
            stack[z, y] = spread(values[:, :NX])
            stack[z, y + 1] = spread(values[:, NX:])
        return carry

    lax.fori_loop(0, planes, lift_plane, 0)
    conv_rows(stack, fine, acc)
    for z in range(CZ):
        for j in range(YT // 2):
            values = act(acc[z, j]).astype(BF16)
            second[z, 2 * j] = values[:, :NX]
            second[z, 2 * j + 1] = values[:, NX:]
    source = lax.broadcasted_iota(jnp.int32, (NX, NX), 0)
    target = lax.broadcasted_iota(jnp.int32, (NX, NX), 1)
    half = NX // 2
    parity = jnp.where(target < half, 0, 1)
    sel = jnp.where(source == 2 * (target - half * parity) + parity, 1.0, 0.0).astype(BF16)
    chans = down.shape[0] // 2
    lane = lane_index(chans // 2)
    for z in range(CZ // 2):
        for j in range(YT // 4):
            pair = []
            for y in (2 * j, 2 * j + 1):
                tall = jnp.concatenate(
                    [second[2 * z + a, 2 * y + b] for a in range(2) for b in range(2)], 0
                )
                pair.append(dot(tall, sel).astype(BF16))
            out = dot(down[...], jnp.concatenate(pair, 1))
            for s in range(2):
                q = out[:, s * NX : (s + 1) * NX]
                h = chans // 2
                q00, q01, q10, q11 = (q[i * h : (i + 1) * h] for i in range(4))
                row = jnp.where(lane < half, q00, q11) + pltpu.roll(
                    jnp.where(lane < half, q01, q10), half, 1
                )
                lowered[z, 2 * j + s] = act(row).astype(BF16)


def coarse_kernel(low, weight, up, second, joined, acc):
    half = NX // 2
    chans = weight.shape[2]
    outs = up.shape[3]
    lane = lane_index(chans // 2)
    planes = low.shape[0]
    for z in range(planes):
        row = [low[z, y].astype(F32) for y in range(low.shape[1])]
        turned = [pltpu.roll(r, half, 1) for r in row]
        pairs = []
        for r in range(len(row) - 1):
            top = jnp.where(lane < half, row[r], turned[r + 1])
            bottom = jnp.where(lane < half, turned[r], row[r + 1])
            pairs.append(jnp.concatenate([top, bottom], 0).astype(BF16))
        for b in range(3):
            right = jnp.concatenate([pairs[b], pairs[2 + b]], 1)
            for a in range(3):
                if 0 <= z - a < planes - 2:
                    for k in range(3):
                        part = dot(weight[a, b, :, k * chans : (k + 1) * chans], right)
                        if a == 0 and b == 0:
                            acc[z - a, k] = part
                        else:
                            acc[z - a, k] += part
    source = lax.broadcasted_iota(jnp.int32, (NX, 4 * NX), 0)
    target = lax.broadcasted_iota(jnp.int32, (NX, 4 * NX), 1)
    spot = target % NX
    want = target // (2 * NX) * half + spot // 2
    sel = jnp.where((source == want) & (spot % 2 == target // NX % 2), 1.0, 0.0).astype(BF16)
    lane = lane_index(chans)
    lefts = [
        jnp.concatenate([up[a, b, k] for a in range(2) for b in range(2)], 0) for k in range(2)
    ]
    for z in range(planes - 2):
        for j in range(2):
            at = slice(j * NX, (j + 1) * NX)
            before, same, after = (acc[z, k, :, at] for k in range(3))
            before = jnp.where(
                lane % half == 0, pltpu.roll(before, half + 1, 1), pltpu.roll(before, 1, 1)
            )
            after = jnp.where(
                lane % half == half - 1,
                pltpu.roll(after, half - 1, 1),
                pltpu.roll(after, NX - 1, 1),
            )
            coarse = act(before + same + after).astype(BF16)
            wide = dot(coarse, sel).astype(BF16)
            right = [
                jnp.concatenate([wide[:, k * NX : (k + 1) * NX], wide[:, (2 + k) * NX : (3 + k) * NX]], 1)
                for k in range(2)
            ]
            raised = dot(lefts[0], right[0]) + dot(lefts[1], right[1])
            for a in range(2):
                for b in range(2):
                    for p in range(2):
                        y = 2 * (2 * j + p) + b
                        piece = raised[
                            (2 * a + b) * outs : (2 * a + b + 1) * outs, p * NX : (p + 1) * NX
                        ]
                        joined[2 * z + a, y] = (second[2 * z + a, y].astype(F32) + piece).astype(
                            BF16
                        )


def middle_kernel(bits, count, field, lift_raw, fine, down_raw, coarse_far, up, out, *scratch):
    first, (grid, second, lowered, low, joined, wide, stack, acc, lift, down) = (
        scratch[:count],
        scratch[count : count + 10],
    )
    total, coarse, send_a, recv_a, send_b, recv_b, fetched = scratch[count + 10 :]
    fetch = pltpu.make_async_copy(coarse_far, coarse, fetched)
    fetch.start()
    meet(bits)
    reduce_stage(bits, field, grid, *first)
    fine_kernel(grid, lift_raw, fine, down_raw, second, lowered, wide, stack, acc, lift, down)
    exchange(lowered, low, 1, send_a, recv_a)
    fetch.wait()
    coarse_kernel(low, coarse, up, second, joined, total)
    exchange(joined, out, 1, send_b, recv_b)


def middle(field, lift, fine, down, coarse, up):
    attrs, slabs, tiles, size, lanes = field.shape
    bits = slabs.bit_length() - 1
    outs, chans = fine.shape[2], coarse.shape[2]
    parts = [
        pltpu.VMEM((attrs,) + (2,) * (bits - 1 - stage) + (tiles, size, lanes), BF16)
        for stage in range(bits)
    ]
    eight = pltpu.SemaphoreType.DMA((8,))
    first = parts + parts
    first += [
        pltpu.VMEM((attrs, tiles - 1, size, lanes), BF16),
        pltpu.VMEM((CZ, YT, 8, lanes), F32),
        pltpu.SemaphoreType.DMA((bits, attrs)),
        pltpu.SemaphoreType.DMA((bits, attrs)),
        pltpu.SemaphoreType.DMA((attrs, tiles - 1)),
        pltpu.SemaphoreType.DMA((attrs, tiles - 1)),
        eight,
        eight,
    ]
    planes, rows = CZ + 2, YT + 2
    rest = [
        pltpu.VMEM((planes + 2, rows + 2, 8, lanes), F32),
        pltpu.VMEM((CZ, YT, outs, lanes), BF16),
        pltpu.VMEM((CZ // 2, YT // 2, chans // 2, lanes), BF16),
        pltpu.VMEM((CZ // 2 + 2, YT // 2 + 2, chans // 2, lanes), BF16),
        pltpu.VMEM((CZ, YT, outs, lanes), BF16),
        pltpu.VMEM((planes + 2, rows + 2, 24, lanes), F32),
        pltpu.VMEM((planes, rows, 3 * outs, lanes), BF16),
        pltpu.VMEM((CZ, YT // 2, outs, 2 * lanes), F32),
        pltpu.VMEM((outs, 216), BF16),
        pltpu.VMEM((2 * chans, 4 * outs), BF16),
        pltpu.VMEM((CZ // 2, 3, chans, 2 * lanes), F32),
        pltpu.VMEM(coarse.shape, BF16),
        eight,
        eight,
        eight,
        eight,
        pltpu.SemaphoreType.DMA,
    ]
    near = pl.BlockSpec(memory_space=pltpu.VMEM)
    return pl.pallas_call(
        functools.partial(middle_kernel, bits, len(first)),
        in_specs=[near, near, near, near, pl.BlockSpec(memory_space=pl.ANY), near],
        out_specs=near,
        out_shape=jax.ShapeDtypeStruct((planes, rows, outs, lanes), BF16),
        scratch_shapes=first + rest,
        compiler_params=pltpu.CompilerParams(
            collective_id=0, has_side_effects=True, vmem_limit_bytes=56 << 20
        ),
        name="middle",
    )(
        field.reshape((attrs,) + (2,) * bits + field.shape[2:]),
        lift.swapaxes(2, 3),
        fine,
        down.swapaxes(3, 4),
        coarse,
        up,
    )


def merge_kernel(joined, weight, head, out, stack, acc):
    planes, rows = joined.shape[:2]

    def widen(z, carry):
        for y in range(rows):
            stack[z, y] = spread(joined[z, y].astype(F32))
        return carry

    lax.fori_loop(0, planes, widen, 0)
    conv_rows(stack, weight, acc)
    for z in range(planes - 2):
        for j in range(rows // 2 - 1):
            moved = dot(head[...], act(acc[z, j]).astype(BF16))
            for s in range(2):
                out[:, z, 2 * j + s, :] = moved[: out.shape[0], s * NX : (s + 1) * NX]


def merge_level(joined, weight, head):
    planes, rows, chans, lanes = joined.shape
    final = head.shape[0]
    return pl.pallas_call(
        merge_kernel,
        out_shape=jax.ShapeDtypeStruct((final, planes - 2, rows - 2, lanes), F32),
        scratch_shapes=[
            pltpu.VMEM((planes, rows, 3 * chans, lanes), BF16),
            pltpu.VMEM((planes - 2, rows // 2 - 1, chans, 2 * lanes), F32),
        ],
        compiler_params=pltpu.CompilerParams(vmem_limit_bytes=48 << 20),
        name="merge_level",
    )(joined, weight, head)


GROUP = 8
CHUNK = 512


def deposit_kernel(slabs, tiles, feat_ref, dest_ref, cell_ref, code_ref, live_ref, out_ref, right, acc):
    group = pl.program_id(0)
    rows = feat_ref.shape[1]
    attrs = feat_ref.shape[0]
    ny = tiles * YT
    nz = slabs * CZ
    f32 = jnp.float32

    @pl.when(group == 0)
    def _():
        def build(j, carry):
            at = pl.ds(pl.multiple_of(j * CHUNK, CHUNK), CHUNK)
            cells = cell_ref[:, at]
            codes = code_ref[:, at]
            lane = lax.broadcasted_iota(jnp.int32, (1, CHUNK), 1) + j * CHUNK
            live = lane < live_ref[0]
            feats = jnp.where(live, feat_ref[:, at].astype(f32), 0.0)
            frac = (codes & 63).astype(f32) * (1.0 / 64.0)
            col = cells & (NX - 1)
            nxt = (col + 1) & (NX - 1)
            xs = lax.broadcasted_iota(jnp.int32, (NX, CHUNK), 0)
            wx = jnp.where(xs == col, 1.0 - frac, 0.0) + jnp.where(xs == nxt, frac, 0.0)
            for c in range(attrs):
                right[c * NX : (c + 1) * NX, at] = (wx * feats[c : c + 1, :]).astype(jnp.bfloat16)
            return carry

        lax.fori_loop(0, rows // CHUNK, build, 0)

    def step(j, carry):
        at = pl.ds(pl.multiple_of(j * CHUNK, CHUNK), CHUNK)
        cells = cell_ref[:, at]
        codes = code_ref[:, at]
        fz = ((codes >> 12) & 63).astype(f32) * (1.0 / 64.0)
        fy = ((codes >> 6) & 63).astype(f32) * (1.0 / 64.0)
        row = cells // NX
        y0 = row % ny
        z0 = dest_ref[:, at] * CZ + row // ny
        y1 = (y0 + 1) % ny
        z1 = (z0 + 1) % nz
        ys = lax.broadcasted_iota(jnp.int32, (ny, CHUNK), 0)
        wy = jnp.where(ys == y0, 1.0 - fy, 0.0) + jnp.where(ys == y1, fy, 0.0)
        zs = lax.broadcasted_iota(jnp.int32, (GROUP * CZ, CHUNK), 0) + group * GROUP * CZ
        wz = jnp.where(zs == z0, 1.0 - fz, 0.0) + jnp.where(zs == z1, fz, 0.0)
        pieces = []
        for s in range(GROUP):
            for t in range(tiles):
                for z in range(CZ):
                    k = s * CZ + z
                    pieces.append(wz[k : k + 1, :] * wy[t * YT : (t + 1) * YT, :])
        left = jnp.concatenate(pieces, 0).astype(jnp.bfloat16)
        part = lax.dot_general(
            left, right[:, at], (((1,), (1,)), ((), ())), preferred_element_type=f32
        )

        @pl.when(j == 0)
        def _():
            acc[...] = part

        @pl.when(j > 0)
        def _():
            acc[...] += part

        return carry

    lax.fori_loop(0, rows // CHUNK, step, 0)
    size = CZ * YT
    for s in range(GROUP):
        for t in range(tiles):
            k = (s * tiles + t) * size
            for c in range(attrs):
                out_ref[c, s, t] = acc[k : k + size, c * NX : (c + 1) * NX].astype(jnp.bfloat16)


def deposit(features, destination, cell_index, offset_code, live_count, slabs, tiles):
    attrs, rows = features.shape
    size = CZ * YT
    whole = lambda shape: pl.BlockSpec(shape, lambda g: (0, 0))
    return pl.pallas_call(
        functools.partial(deposit_kernel, slabs, tiles),
        grid=(slabs // GROUP,),
        in_specs=[
            whole((attrs, rows)),
            whole((1, rows)),
            whole((1, rows)),
            whole((1, rows)),
            pl.BlockSpec(memory_space=pltpu.SMEM),
        ],
        out_specs=pl.BlockSpec((attrs, GROUP, tiles, size, NX), lambda g: (0, g, 0, 0, 0)),
        out_shape=jax.ShapeDtypeStruct((attrs, slabs, tiles, size, NX), jnp.bfloat16),
        scratch_shapes=[
            pltpu.VMEM((attrs * NX, rows), jnp.bfloat16),
            pltpu.VMEM((GROUP * tiles * size, attrs * NX), jnp.float32),
        ],
        compiler_params=pltpu.CompilerParams(vmem_limit_bytes=60 << 20),
        name="deposit",
    )(
        features,
        destination.reshape(1, rows),
        cell_index.reshape(1, rows),
        offset_code.reshape(1, rows),
        live_count,
    )


def body(
    particle_features,
    destination,
    cell_index,
    offset_code,
    live_count,
    lift_weight,
    fine_weight,
    down_weight,
    coarse_weight,
    up_weight,
    merge_weight,
    head_weight,
):
    slabs = lax.axis_size("slab")
    tiles = lax.axis_size("tile")
    field = deposit(
        particle_features, destination, cell_index, offset_code, live_count, slabs, tiles
    )
    joined = middle(field, lift_weight, fine_weight, down_weight, coarse_weight, up_weight)
    return merge_level(joined, merge_weight, head_weight)


def solution(mesh):
    placed = (
        P(None, ("slab", "tile")),
        P(("slab", "tile"), None),
        P(("slab", "tile")),
        P(("slab", "tile")),
        P(("slab", "tile")),
        P(),
        P(),
        P(),
        P(),
        P(),
        P(),
        P(),
    )
    return jax.shard_map(
        body, mesh=mesh, in_specs=placed, out_specs=P(None, "slab", "tile", None), check_vma=False
    )
```

```python
import functools

import jax
import jax.numpy as jnp
from jax import lax
from jax.experimental import pallas as pl
from jax.experimental.pallas import tpu as pltpu
from jax.sharding import PartitionSpec as P

NX = 128
YT = 8
CZ = 4


slope = 0.1


BF16 = jnp.bfloat16
F32 = jnp.float32
MESH = pl.DeviceIdType.MESH
SIDES = [(dz, dy) for dz in (-1, 0, 1) for dy in (-1, 0, 1) if dz or dy]


def act(values):
    return jnp.maximum(values, slope * values)


def dot(left, right):
    return jnp.dot(left, right, preferred_element_type=F32)


def neighbour(dz, dy):
    slabs, tiles = lax.axis_size("slab"), lax.axis_size("tile")
    return (
        lax.rem(lax.axis_index("slab") + (dz + slabs), slabs),
        lax.rem(lax.axis_index("tile") + (dy + tiles), tiles),
    )


def greet(devices):
    barrier = pltpu.get_barrier_semaphore()
    for device in devices:
        pl.semaphore_signal(barrier, inc=1, device_id=device, device_id_type=MESH)
    pl.semaphore_wait(barrier, len(devices))


def span(shift, size, width):
    if shift > 0:
        return pl.ds(size - width, width), pl.ds(0, width)
    if shift < 0:
        return pl.ds(0, width), pl.ds(size + width, width)
    return pl.ds(0, size), pl.ds(width, size)


def exchange(block, padded, width, send, recv):
    planes, rows = block.shape[:2]
    copies = []
    for n, (dz, dy) in enumerate(SIDES):
        from_z, to_z = span(dz, planes, width)
        from_y, to_y = span(dy, rows, width)
        copies.append(
            pltpu.make_async_remote_copy(
                src_ref=block.at[from_z, from_y],
                dst_ref=padded.at[to_z, to_y],
                send_sem=send.at[n],
                recv_sem=recv.at[n],
                device_id=neighbour(dz, dy),
                device_id_type=MESH,
            )
        )
    for copy in copies:
        copy.start()
    padded[pl.ds(width, planes), pl.ds(width, rows)] = block[...]
    for copy in copies:
        copy.wait()


GROUP = 8
CHUNK = 512
DEEP = 1024


def deposit_stage(bits, feat_ref, dest_ref, cell_ref, code_ref, live_ref, field, left, right, acc, ready):
    attrs, rows = feat_ref.shape
    slabs, tiles = 2**bits, field.shape[bits + 1]
    ny = tiles * YT
    nz = slabs * CZ
    f32 = jnp.float32

    def build(j, carry):
        at = pl.ds(pl.multiple_of(j * CHUNK, CHUNK), CHUNK)
        cells = cell_ref[:, at]
        codes = code_ref[:, at]
        lane = lax.broadcasted_iota(jnp.int32, (1, CHUNK), 1) + j * CHUNK
        live = lane < live_ref[0]
        feats = jnp.where(live, feat_ref[:, at].astype(f32), 0.0)
        frac = (codes & 63).astype(f32) * (1.0 / 64.0)
        col = cells & (NX - 1)
        nxt = (col + 1) & (NX - 1)
        xs = lax.broadcasted_iota(jnp.int32, (NX, CHUNK), 0)
        wx = jnp.where(xs == col, 1.0 - frac, 0.0) + jnp.where(xs == nxt, frac, 0.0)
        for c in range(attrs):
            right[c * NX : (c + 1) * NX, at] = (wx * feats[c : c + 1, :]).astype(jnp.bfloat16)
        return carry

    lax.fori_loop(0, rows // CHUNK, build, 0)

    def tall(j, group):
        at = pl.ds(pl.multiple_of(j * CHUNK, CHUNK), CHUNK)
        cells = cell_ref[:, at]
        codes = code_ref[:, at]
        fz = ((codes >> 12) & 63).astype(f32) * (1.0 / 64.0)
        fy = ((codes >> 6) & 63).astype(f32) * (1.0 / 64.0)
        row = cells // NX
        y0 = row % ny
        z0 = dest_ref[:, at] * CZ + row // ny
        y1 = (y0 + 1) % ny
        z1 = (z0 + 1) % nz
        ys = lax.broadcasted_iota(jnp.int32, (ny, CHUNK), 0)
        wy = jnp.where(ys == y0, 1.0 - fy, 0.0) + jnp.where(ys == y1, fy, 0.0)
        zs = lax.broadcasted_iota(jnp.int32, (GROUP * CZ, CHUNK), 0) + group * GROUP * CZ
        wz = jnp.where(zs == z0, 1.0 - fz, 0.0) + jnp.where(zs == z1, fz, 0.0)
        pieces = []
        for s in range(GROUP):
            for t in range(tiles):
                for z in range(CZ):
                    k = s * CZ + z
                    pieces.append(wz[k : k + 1, :] * wy[t * YT : (t + 1) * YT, :])
        left[:, at] = jnp.concatenate(pieces, 0).astype(jnp.bfloat16)
        return group

    size = CZ * YT
    groups = slabs // GROUP
    for group in range(groups):
        lax.fori_loop(0, rows // CHUNK, tall, group)
        for n in range(attrs // 2):
            acc[...] = jnp.zeros_like(acc)

            def step(j, carry):
                at = pl.ds(pl.multiple_of(j * DEEP, DEEP), DEEP)
                acc[...] += lax.dot_general(
                    left[:, at],
                    right[2 * n * NX : (2 * n + 2) * NX, at],
                    (((1,), (1,)), ((), ())),
                    preferred_element_type=f32,
                )
                return carry

            lax.fori_loop(0, rows // DEEP, step, 0)
            for c in range(2):
                for s in range(GROUP):
                    slab = group * GROUP + s
                    spot = tuple(slab // 2**b % 2 for b in range(bits - 1, -1, -1))
                    for t in range(tiles):
                        k = (s * tiles + t) * size
                        field[(2 * n + c,) + spot + (t,)] = acc[
                            k : k + size, c * NX : (c + 1) * NX
                        ].astype(BF16)
                if group == groups - 1:
                    ready(2 * n + c)


def meet(bits):
    slab, tile, tiles = lax.axis_index("slab"), lax.axis_index("tile"), lax.axis_size("tile")
    partner = [(slab + 2**b * (1 - 2 * (slab // 2**b % 2)), tile) for b in range(bits)]
    ahead = [(slab, lax.rem(tile + d, tiles)) for d in range(1, tiles)]
    greet(partner + ahead + [neighbour(dz, dy) for dz, dy in SIDES])


def reduce_stage(bits, fill, field, padded, *scratch):
    tiles = lax.axis_size("tile")
    attrs = field.shape[0]
    slab, tile = lax.axis_index("slab"), lax.axis_index("tile")
    mine = [slab // 2**b % 2 for b in range(bits)]
    partner = [(slab + 2**b * (1 - 2 * mine[b]), tile) for b in range(bits)]
    ahead = [(slab, lax.rem(tile + d, tiles)) for d in range(1, tiles)]
    gets, sums = scratch[:bits], scratch[bits : 2 * bits]
    last, block, send, recv, send_z, recv_z, send_h, recv_h = scratch[2 * bits :]
    orders = [[0] + list(range(1, bits)), [0] + list(range(bits - 1, 0, -1))]

    def part(c, stage, side):
        order = orders[c % 2]
        rest = [b for b in range(bits - 1, -1, -1) if b not in order[:stage]]
        b = order[stage]
        source = field if stage == 0 else sums[stage - 1]
        which = mine[b] if side == 0 else 1 - mine[b]
        return source, (c,) + (slice(None),) * rest.index(b) + (which,)

    def push(c, stage):
        source, at = part(c, stage, 1)
        copy = pltpu.make_async_remote_copy(
            src_ref=source.at[at],
            dst_ref=gets[stage].at[c],
            send_sem=send.at[stage, c],
            recv_sem=recv.at[stage, c],
            device_id=partner[orders[c % 2][stage]],
            device_id_type=MESH,
        )
        copy.start()
        return copy

    def deal(c):
        copies = []
        for d in range(1, tiles):
            copy = pltpu.make_async_remote_copy(
                src_ref=sums[bits - 1].at[c, lax.rem(tile + d, tiles)],
                dst_ref=last.at[c, d - 1],
                send_sem=send_z.at[c, d - 1],
                recv_sem=recv_z.at[c, d - 1],
                device_id=ahead[d - 1],
                device_id_type=MESH,
            )
            copy.start()
            copies.append(copy)
        return copies

    flying = []
    fill(lambda c: flying.append(push(c, 0)))
    for stage in range(bits):
        for c in range(attrs):
            flying[c].wait()
            source, at = part(c, stage, 0)
            total = source[at].astype(F32) + gets[stage][c].astype(F32)
            sums[stage][c] = total.astype(BF16)
            flying[c] = push(c, stage + 1) if stage < bits - 1 else deal(c)
    block[...] = jnp.zeros_like(block)
    for c in range(attrs):
        total = sums[bits - 1][c, tile].astype(F32)
        for d in range(1, tiles):
            flying[c][d - 1].wait()
            total = total + last[c, d - 1].astype(F32)
        total = total.astype(BF16).astype(F32)
        for z in range(CZ):
            block[z, :, c, :] = total[z * YT : (z + 1) * YT]
    exchange(block, padded, 2, send_h, recv_h)


def spread(values):
    return jnp.concatenate(
        [pltpu.roll(values, 1, 1), values, pltpu.roll(values, NX - 1, 1)], 0
    ).astype(BF16)


def conv_rows(stack, weight, acc):
    planes, rows = stack.shape[0] - 2, stack.shape[1] - 2
    outs = weight.shape[2]
    lefts = [jnp.concatenate([weight[a, b] for a in range(3)], 0) for b in range(3)]
    for z in range(planes + 2):
        for j in range(rows // 2):
            part = None
            for b in range(3):
                y = 2 * j + b
                pair = jnp.concatenate([stack[z, y], stack[z, y + 1]], 1)
                term = dot(lefts[b], pair)
                part = term if part is None else part + term
            for a in range(3):
                if 0 <= z - a < planes:
                    piece = part[a * outs : (a + 1) * outs]
                    if a == 0:
                        acc[z, j] = piece
                    else:
                        acc[z - a, j] += piece


def lane_index(rows):
    return lax.broadcasted_iota(jnp.int32, (rows, 128), 1)


def cross(left, right):
    return lax.dot_general(left, right, (((0,), (0,)), ((), ())), preferred_element_type=F32)


def place(rows, columns, target_of):
    source = lax.broadcasted_iota(jnp.int32, (rows, columns), 0)
    target = lax.broadcasted_iota(jnp.int32, (rows, columns), 1)
    return jnp.where(target == target_of(source), 1.0, 0.0).astype(BF16)


def fine_kernel(grid, lift_raw, fine, down_raw, second, lowered, wide, stack, acc, lift, down):
    planes, rows = grid.shape[0] - 2, grid.shape[1] - 2
    taps = lift_raw.shape[2]
    each = taps // 3
    total = None
    for n in range(9):
        spots = place(taps, 216, lambda i: n * 24 + i // each * 8 + i % each)
        term = cross(lift_raw[n // 3, n % 3], spots)
        total = term if total is None else total + term
    lift[...] = total.astype(BF16)
    depth, tall = down_raw.shape[3:]
    for k in range(2):
        total = None
        for n in range(4):
            spots = place(depth, 4 * depth, lambda i: n * depth + i)
            term = cross(down_raw[n // 2, n % 2, k], spots)
            total = term if total is None else total + term
        down[k * tall : (k + 1) * tall] = total.astype(BF16)
    for z in range(planes + 2):
        block = grid[z]
        wide[z, :, 0:8] = pltpu.roll(block, 1, 2)
        wide[z, :, 8:16] = block
        wide[z, :, 16:24] = pltpu.roll(block, NX - 1, 2)

    def lift_plane(z, carry):
        for y in range(0, rows, 2):
            pair = jnp.concatenate(
                [
                    jnp.concatenate(
                        [wide[z + a, y + s + b] for a in range(3) for b in range(3)], 0
                    ).astype(BF16)
                    for s in range(2)
                ],
                1,
            )
            values = act(dot(lift[...], pair))
            stack[z, y] = spread(values[:, :NX])
            stack[z, y + 1] = spread(values[:, NX:])
        return carry

    lax.fori_loop(0, planes, lift_plane, 0)
    conv_rows(stack, fine, acc)
    for z in range(CZ):
        for j in range(YT // 2):
            values = act(acc[z, j]).astype(BF16)
            second[z, 2 * j] = values[:, :NX]
            second[z, 2 * j + 1] = values[:, NX:]
    source = lax.broadcasted_iota(jnp.int32, (NX, NX), 0)
    target = lax.broadcasted_iota(jnp.int32, (NX, NX), 1)
    half = NX // 2
    parity = jnp.where(target < half, 0, 1)
    sel = jnp.where(source == 2 * (target - half * parity) + parity, 1.0, 0.0).astype(BF16)
    chans = down.shape[0] // 2
    lane = lane_index(chans // 2)
    for z in range(CZ // 2):
        for j in range(YT // 4):
            pair = []
            for y in (2 * j, 2 * j + 1):
                tall = jnp.concatenate(
                    [second[2 * z + a, 2 * y + b] for a in range(2) for b in range(2)], 0
                )
                pair.append(dot(tall, sel).astype(BF16))
            out = dot(down[...], jnp.concatenate(pair, 1))
            for s in range(2):
                q = out[:, s * NX : (s + 1) * NX]
                h = chans // 2
                q00, q01, q10, q11 = (q[i * h : (i + 1) * h] for i in range(4))
                row = jnp.where(lane < half, q00, q11) + pltpu.roll(
                    jnp.where(lane < half, q01, q10), half, 1
                )
                lowered[z, 2 * j + s] = act(row).astype(BF16)


def coarse_kernel(low, weight, up, second, joined, acc):
    half = NX // 2
    chans = weight.shape[2]
    outs = up.shape[3]
    lane = lane_index(chans // 2)
    planes = low.shape[0]
    for z in range(planes):
        row = [low[z, y].astype(F32) for y in range(low.shape[1])]
        turned = [pltpu.roll(r, half, 1) for r in row]
        pairs = []
        for r in range(len(row) - 1):
            top = jnp.where(lane < half, row[r], turned[r + 1])
            bottom = jnp.where(lane < half, turned[r], row[r + 1])
            pairs.append(jnp.concatenate([top, bottom], 0).astype(BF16))
        for b in range(3):
            right = jnp.concatenate([pairs[b], pairs[2 + b]], 1)
            for a in range(3):
                if 0 <= z - a < planes - 2:
                    for k in range(3):
                        part = dot(weight[a, b, :, k * chans : (k + 1) * chans], right)
                        if a == 0 and b == 0:
                            acc[z - a, k] = part
                        else:
                            acc[z - a, k] += part
    source = lax.broadcasted_iota(jnp.int32, (NX, 4 * NX), 0)
    target = lax.broadcasted_iota(jnp.int32, (NX, 4 * NX), 1)
    spot = target % NX
    want = target // (2 * NX) * half + spot // 2
    sel = jnp.where((source == want) & (spot % 2 == target // NX % 2), 1.0, 0.0).astype(BF16)
    lane = lane_index(chans)
    lefts = [
        jnp.concatenate([up[a, b, k] for a in range(2) for b in range(2)], 0) for k in range(2)
    ]
    for z in range(planes - 2):
        for j in range(2):
            at = slice(j * NX, (j + 1) * NX)
            before, same, after = (acc[z, k, :, at] for k in range(3))
            before = jnp.where(
                lane % half == 0, pltpu.roll(before, half + 1, 1), pltpu.roll(before, 1, 1)
            )
            after = jnp.where(
                lane % half == half - 1,
                pltpu.roll(after, half - 1, 1),
                pltpu.roll(after, NX - 1, 1),
            )
            coarse = act(before + same + after).astype(BF16)
            wide = dot(coarse, sel).astype(BF16)
            right = [
                jnp.concatenate([wide[:, k * NX : (k + 1) * NX], wide[:, (2 + k) * NX : (3 + k) * NX]], 1)
                for k in range(2)
            ]
            raised = dot(lefts[0], right[0]) + dot(lefts[1], right[1])
            for a in range(2):
                for b in range(2):
                    for p in range(2):
                        y = 2 * (2 * j + p) + b
                        piece = raised[
                            (2 * a + b) * outs : (2 * a + b + 1) * outs, p * NX : (p + 1) * NX
                        ]
                        joined[2 * z + a, y] = (second[2 * z + a, y].astype(F32) + piece).astype(
                            BF16
                        )


def middle_kernel(bits, count, feat, dest, cell, code, live, *rest):
    lift_raw, fine, down_raw, coarse_far, up, out = rest[:6]
    field, left, right, part, *scratch = rest[6:]
    first, (grid, second, lowered, low, joined, wide, stack, acc, lift, down) = (
        scratch[:count],
        scratch[count : count + 10],
    )
    total, coarse, send_a, recv_a, send_b, recv_b, fetched = scratch[count + 10 :]
    fetch = pltpu.make_async_copy(coarse_far, coarse, fetched)
    fetch.start()
    meet(bits)
    fill = functools.partial(
        deposit_stage, bits, feat, dest, cell, code, live, field, left, right, part
    )
    reduce_stage(bits, fill, field, grid, *first)
    fine_kernel(grid, lift_raw, fine, down_raw, second, lowered, wide, stack, acc, lift, down)
    exchange(lowered, low, 1, send_a, recv_a)
    fetch.wait()
    coarse_kernel(low, coarse, up, second, joined, total)
    exchange(joined, out, 1, send_b, recv_b)


def middle(features, destination, cells, codes, live, lift, fine, down, coarse, up):
    attrs, total = features.shape
    slabs, tiles = lax.axis_size("slab"), lax.axis_size("tile")
    size, lanes = CZ * YT, NX
    bits = slabs.bit_length() - 1
    outs, chans = fine.shape[2], coarse.shape[2]
    parts = [
        pltpu.VMEM((attrs,) + (2,) * (bits - 1 - stage) + (tiles, size, lanes), BF16)
        for stage in range(bits)
    ]
    eight = pltpu.SemaphoreType.DMA((8,))
    first = parts + parts
    first += [
        pltpu.VMEM((attrs, tiles - 1, size, lanes), BF16),
        pltpu.VMEM((CZ, YT, 8, lanes), F32),
        pltpu.SemaphoreType.DMA((bits, attrs)),
        pltpu.SemaphoreType.DMA((bits, attrs)),
        pltpu.SemaphoreType.DMA((attrs, tiles - 1)),
        pltpu.SemaphoreType.DMA((attrs, tiles - 1)),
        eight,
        eight,
    ]
    planes, rows = CZ + 2, YT + 2
    tall = GROUP * tiles * size
    early = [
        pltpu.VMEM((attrs,) + (2,) * bits + (tiles, size, lanes), BF16),
        pltpu.VMEM((tall, total), BF16),
        pltpu.VMEM((attrs * lanes, total), BF16),
        pltpu.VMEM((tall, 2 * lanes), F32),
    ]
    rest = [
        pltpu.VMEM((planes + 2, rows + 2, 8, lanes), F32),
        pltpu.VMEM((CZ, YT, outs, lanes), BF16),
        pltpu.VMEM((CZ // 2, YT // 2, chans // 2, lanes), BF16),
        pltpu.VMEM((CZ // 2 + 2, YT // 2 + 2, chans // 2, lanes), BF16),
        pltpu.VMEM((CZ, YT, outs, lanes), BF16),
        pltpu.VMEM((planes + 2, rows + 2, 24, lanes), F32),
        pltpu.VMEM((planes, rows, 3 * outs, lanes), BF16),
        pltpu.VMEM((CZ, YT // 2, outs, 2 * lanes), F32),
        pltpu.VMEM((outs, 216), BF16),
        pltpu.VMEM((2 * chans, 4 * outs), BF16),
        pltpu.VMEM((CZ // 2, 3, chans, 2 * lanes), F32),
        pltpu.VMEM(coarse.shape, BF16),
        eight,
        eight,
        eight,
        eight,
        pltpu.SemaphoreType.DMA,
    ]
    near = pl.BlockSpec(memory_space=pltpu.VMEM)
    return pl.pallas_call(
        functools.partial(middle_kernel, bits, len(first)),
        in_specs=[near] * 4
        + [pl.BlockSpec(memory_space=pltpu.SMEM)]
        + [near] * 3
        + [pl.BlockSpec(memory_space=pl.ANY), near],
        out_specs=near,
        out_shape=jax.ShapeDtypeStruct((planes, rows, outs, lanes), BF16),
        scratch_shapes=early + first + rest,
        compiler_params=pltpu.CompilerParams(
            collective_id=0, has_side_effects=True, vmem_limit_bytes=60 << 20
        ),
        name="middle",
    )(
        features,
        destination.reshape(1, total),
        cells.reshape(1, total),
        codes.reshape(1, total),
        live,
        lift.swapaxes(2, 3),
        fine,
        down.swapaxes(3, 4),
        coarse,
        up,
    )


def merge_kernel(joined, weight, head, out, stack, acc):
    planes, rows = joined.shape[:2]

    def widen(z, carry):
        for y in range(rows):
            stack[z, y] = spread(joined[z, y].astype(F32))
        return carry

    lax.fori_loop(0, planes, widen, 0)
    conv_rows(stack, weight, acc)
    for z in range(planes - 2):
        for j in range(rows // 2 - 1):
            moved = dot(head[...], act(acc[z, j]).astype(BF16))
            for s in range(2):
                out[:, z, 2 * j + s, :] = moved[: out.shape[0], s * NX : (s + 1) * NX]


def merge_level(joined, weight, head):
    planes, rows, chans, lanes = joined.shape
    final = head.shape[0]
    return pl.pallas_call(
        merge_kernel,
        out_shape=jax.ShapeDtypeStruct((final, planes - 2, rows - 2, lanes), F32),
        scratch_shapes=[
            pltpu.VMEM((planes, rows, 3 * chans, lanes), BF16),
            pltpu.VMEM((planes - 2, rows // 2 - 1, chans, 2 * lanes), F32),
        ],
        compiler_params=pltpu.CompilerParams(vmem_limit_bytes=48 << 20),
        name="merge_level",
    )(joined, weight, head)


def body(
    particle_features,
    destination,
    cell_index,
    offset_code,
    live_count,
    lift_weight,
    fine_weight,
    down_weight,
    coarse_weight,
    up_weight,
    merge_weight,
    head_weight,
):
    joined = middle(
        particle_features,
        destination,
        cell_index,
        offset_code,
        live_count,
        lift_weight,
        fine_weight,
        down_weight,
        coarse_weight,
        up_weight,
    )
    return merge_level(joined, merge_weight, head_weight)


def solution(mesh):
    placed = (
        P(None, ("slab", "tile")),
        P(("slab", "tile"), None),
        P(("slab", "tile")),
        P(("slab", "tile")),
        P(("slab", "tile")),
        P(),
        P(),
        P(),
        P(),
        P(),
        P(),
        P(),
    )
    return jax.shard_map(
        body, mesh=mesh, in_specs=placed, out_specs=P(None, "slab", "tile", None), check_vma=False
    )
```
